256 devices in a mesh: expert: 128 (over x, z, y), half: 2 (over core).
Axes of the slice: x: 4, y: 4, z: 8, core: 2. Of those that a mesh axis runs over, the one named last changes fastest.
Arguments:
- tokens: bfloat16 [8192, 2048], P('expert'), may hold values from -6 to 6
- routes: int32 [8192, 8], P('expert'), may hold values from 0 to 127, all different within a row; in each aligned block of 64 rows (0 to 63, 64 to 127, ...) at most 8 rows name the same one
- gates: float32 [8192, 8], P('expert'), may hold values from 0.05 to 0.5
- cotangent: bfloat16 [8192, 2048], P('expert'), may hold values from -1.5 to 1.5
- w_gate: bfloat16 [128, 2048, 768], P('expert', None, 'half'), may hold values from -0.125 to 0.125
- w_up: bfloat16 [128, 2048, 768], P('expert', None, 'half'), may hold values from -0.125 to 0.125
- w_down: bfloat16 [128, 768, 2048], P('expert', 'half'), may hold values from -0.21875 to 0.21875
Outputs:
- mixed: bfloat16 [8192, 2048], P('expert')
- token_grad: bfloat16 [8192, 2048], P('expert')
- gate_grad: float32 [8192, 8], P('expert')
- grad_gate: bfloat16 [128, 2048, 768], P('expert', None, 'half')
- grad_up: bfloat16 [128, 2048, 768], P('expert', None, 'half')
- grad_down: bfloat16 [128, 768, 2048], P('expert', 'half')
The draws below stay inside these ranges and needn't reach their ends.
Inputs may be any that keep to these rules, and one draw needn't show every extreme that they name: `routes`: each token names 8 different experts. Among the 64 tokens of one index of the expert axis, no expert is named more than 8 times, a bound that some block reaches.
All inputs are finite; a program needn't handle non-finite values.
Results may differ from the reference program's by a relative error of at most 0.0064.
Values may be sent and summed in bfloat16 or wider, within the bound.
A program may use at most 128 MiB of HBM per device.

```python
import math
import jax
import jax.numpy as jnp
import numpy as np
from jax import lax

D = 2048
HID = 768
TOP = 8
TOK_DEV = 64
EXPERTS = 128
CAP = 8
TOKENS = 8192
N_EXPERT = 128


def level_of(stream_key, shape, shards, low, largest):
    level, own = 1.0, jax.random.fold_in(stream_key, 6)
    for axis_at, shards_of in shards:
        heights = jnp.exp(jax.random.uniform(jax.random.fold_in(own, axis_at), (shards_of,), jnp.float32, low / len(shards), largest / len(shards)))
        level = level * jnp.repeat(heights, shape[axis_at] // shards_of).reshape([-1 if axis == axis_at else 1 for axis in range(len(shape))])
    return level


def shared_out(stream_key, own, number, rows, number_of, top, limit, skew):
    sequence = jax.random.permutation(stream_key, number_of)
    heavy_load, usual = load_shares(number_of, rows * top, limit, skew, True), load_shares(number_of, rows * top, limit, skew, False)
    places = jnp.arange(number_of)

    def named(sizes, rotation):
        used = int((sizes > 0).sum())
        fixed = max(1, used // 4)
        shifted = fixed + (places - fixed + rotation * (used - fixed)) % max(1, number_of - fixed)
        return jnp.zeros((number_of,), jnp.int32).at[sequence[jnp.where(places < fixed, places, shifted)]].set(jnp.asarray(sizes, jnp.int32))

    sizes = jnp.where(number % 4 == 0, named(heavy_load, number // 4), named(usual, number - number // 4 - 1))
    mixed = jax.random.permutation(jax.random.fold_in(own, 3), number_of)
    donor, sink = mixed[0:number_of // 2 * 2:2], mixed[1:number_of // 2 * 2:2]
    room = jnp.minimum(sizes[donor] - 1, limit - sizes[sink]) // 2
    room = jnp.where((donor == sequence[0]) | (sink == sequence[0]) | (sizes[sink] == 0), 0, jnp.maximum(room, 0))
    shifted = jax.random.randint(jax.random.fold_in(own, 4), (number_of // 2,), 0, 1 << 20) % (room + 1)
    sizes = sizes.at[donor].add(-shifted).at[sink].add(shifted)
    items = jnp.searchsorted(jnp.cumsum(sizes), jnp.arange(rows * top), side="right").astype(jnp.int32)
    table = items.reshape(top, rows).T
    table = table[jax.random.permutation(jax.random.fold_in(own, 1), rows)]
    rotation = jax.random.randint(jax.random.fold_in(own, 2), (rows, 1), 0, top)
    return jnp.take_along_axis(table, (jnp.arange(top)[None, :] + rotation) % top, axis=1)


def load_shares(amount, total, bound, slope, full):
    portions = [(1 << 20) // math.isqrt(rank ** slope) + 1 for rank in range(1, amount + 1)]
    largest = bound if full else min(bound, max(-(-total // amount), total * portions[0] // sum(portions)))
    least = 1 if total - largest >= amount - 1 else 0
    given, spare = [largest] + [least] * (amount - 1), total - largest - least * (amount - 1)
    while spare > 0:
        movable = [i for i in range(1, amount) if given[i] < largest] or [i for i in range(1, amount) if given[i] < bound]
        mass, left = sum([portions[i] for i in movable]), spare
        for i in movable:
            extra = min(bound - given[i], max(1, left * portions[i] // mass), spare)
            given[i] = given[i] + extra
            spare = spare - extra
    return np.array(given)


def gaussian(own_key, dims, width, reach, pieces=(), kind=jnp.bfloat16):
    level = level_of(own_key, dims, pieces, -0.22, 0.18) if pieces else 1.0
    array = jax.random.normal(own_key, dims, jnp.float32) * width * level
    return jnp.minimum(jnp.maximum(array, -reach), reach).astype(kind)


def setup_inputs(seed: int = 0) -> dict:
    keys = jax.random.split(jax.random.key(seed), 8)
    tokens = gaussian(keys[0], (TOKENS, D), 1.0, 6.0, ((0, 128),))
    routes_keys = jax.random.split(jax.random.fold_in(keys[1], 1), TOKENS // TOK_DEV)
    routes_turns = jax.random.permutation(jax.random.fold_in(keys[1], 3), TOKENS // TOK_DEV)
    routes = jax.vmap(lambda own, number: shared_out(jax.random.fold_in(keys[1], 2), own, number, TOK_DEV, EXPERTS, TOP, CAP, 2))(routes_keys, routes_turns).reshape((TOKENS, TOP))
    gates = jnp.clip(jnp.exp(math.log(0.5) - 2.3025851 * jax.random.uniform(keys[2], (TOKENS, TOP), jnp.float32) ** level_of(keys[2], (TOKENS, TOP), ((0, 128),), -0.2, 0.2)), 0.05, 0.5)
    cotangent = gaussian(keys[3], (TOKENS, D), 0.25, 1.5, ((0, 128),))
    w_gate = gaussian(keys[4], (EXPERTS, D, HID), D ** -0.5, 0.125, ((0, 128), (2, 2)))
    w_up = gaussian(keys[5], (EXPERTS, D, HID), D ** -0.5, 0.125, ((0, 128), (2, 2)))
    w_down = gaussian(keys[6], (EXPERTS, HID, D), HID ** -0.5, 0.21875, ((0, 128), (1, 2)))
    return dict(tokens=tokens, routes=routes, gates=gates, cotangent=cotangent, w_gate=w_gate, w_up=w_up, w_down=w_down)


def expert_pass(rows, scaled, wgate, wupper, wdown):
    pre_gate = jnp.dot(rows, wgate, preferred_element_type=jnp.float32)
    pre_up = jnp.dot(rows, wupper, preferred_element_type=jnp.float32)
    sigma = jax.nn.sigmoid(pre_gate)
    hidden = (pre_gate * sigma * pre_up).astype(jnp.bfloat16)
    expert_out = jnp.dot(hidden, wdown, preferred_element_type=jnp.float32).astype(jnp.bfloat16)
    back_hidden = jnp.dot(scaled, wdown.T, preferred_element_type=jnp.float32)
    d_up = (back_hidden * pre_gate * sigma).astype(jnp.bfloat16)
    d_gate = (back_hidden * pre_up * sigma * (1.0 + pre_gate * (1.0 - sigma))).astype(jnp.bfloat16)
    slot_grad = jnp.dot(d_gate, wgate.T, preferred_element_type=jnp.float32)
    slot_grad = (slot_grad + jnp.dot(d_up, wupper.T, preferred_element_type=jnp.float32)).astype(jnp.bfloat16)
    grad_gate = jnp.dot(rows.T, d_gate, preferred_element_type=jnp.float32).astype(jnp.bfloat16)
    grad_up = jnp.dot(rows.T, d_up, preferred_element_type=jnp.float32).astype(jnp.bfloat16)
    grad_down = jnp.dot(hidden.T, scaled, preferred_element_type=jnp.float32).astype(jnp.bfloat16)
    return expert_out, slot_grad, grad_gate, grad_up, grad_down


def reference(tokens, routes, gates, cotangent, w_gate, w_up, w_down):
    slot_count = TOK_DEV * TOP
    routed = routes.reshape(N_EXPERT, slot_count).astype(jnp.int32)
    expert_ids = jnp.arange(EXPERTS, dtype=jnp.int32)
    onehot = (routed[:, :, None] == expert_ids[None, None, :]).astype(jnp.int32)
    before = (jnp.cumsum(onehot, axis=1) - onehot).astype(jnp.int32)
    placed = jnp.sum(before * onehot, axis=2).astype(jnp.int32)
    source = jnp.broadcast_to(jnp.arange(N_EXPERT, dtype=jnp.int32)[:, None], routed.shape)
    members = jnp.broadcast_to(jnp.arange(slot_count, dtype=jnp.int32)[None, :], routed.shape)
    slot_table = jnp.full((EXPERTS, N_EXPERT, CAP), slot_count, jnp.int32)
    slot_table = slot_table.at[routed, source, placed].set(members)
    gate_flat = gates.reshape(TOKENS * TOP)
    sources = jnp.arange(N_EXPERT, dtype=jnp.int32)[:, None]

    def one_expert(packed):
        lookup, wgate, wupper, wdown = packed
        present = lookup < slot_count
        clipped = jnp.minimum(lookup, slot_count - 1)
        owners = (sources * TOK_DEV + clipped // TOP).astype(jnp.int32)
        gate_index = (sources * slot_count + clipped).astype(jnp.int32)
        rows = jnp.where(present[:, :, None], tokens[owners], jnp.zeros_like(tokens[owners]))
        weighted = gate_flat[gate_index][:, :, None] * cotangent[owners].astype(jnp.float32)
        scaled = jnp.where(present[:, :, None], weighted, 0.0).astype(jnp.bfloat16)
        return expert_pass(rows.reshape(N_EXPERT * CAP, D), scaled.reshape(N_EXPERT * CAP, D), wgate, wupper, wdown)

    outs_all, grads_all, grad_gate, grad_up, grad_down = lax.map(one_expert, (slot_table, w_gate, w_up, w_down))
    position = (source * CAP + placed).astype(jnp.int32)
    out_slots = outs_all[routed, position].reshape(TOKENS, TOP, D).astype(jnp.float32)
    grad_slots = grads_all[routed, position].reshape(TOKENS, TOP, D).astype(jnp.float32)
    mixed = jnp.sum(gates[:, :, None] * out_slots, axis=1).astype(jnp.bfloat16)
    gate_grad = jnp.sum(cotangent.astype(jnp.float32)[:, None, :] * out_slots, axis=2)
    token_grad = jnp.sum(grad_slots, axis=1).astype(jnp.bfloat16)
    return mixed, token_grad, gate_grad, grad_gate, grad_up, grad_down
```

```python
import jax
import jax.numpy as jnp
from jax import lax
from jax.experimental import pallas as pl
from jax.experimental.pallas import tpu as pltpu
from jax.sharding import PartitionSpec as P

MESH = pl.DeviceIdType.MESH
NX, NZ, NY = 4, 8, 4
PLANE = NX * NY
TOK = 64
D = 2048
HALF = D // 2
HID = 384
TOP = 8
CAP = 8
STEPS = 4
ROWS = PLANE * 2 * CAP
OFFSETS = ((-1, 1), (4, -3), (3, -2), (0, 2))
BF = jnp.bfloat16
F32 = jnp.float32


def dot(a, b, ca, cb):
    return lax.dot_general(a, b, (((ca,), (cb,)), ((), ())), preferred_element_type=F32)


def kernel(
    tok, cot, routes, gates, wg_h, wu_h, wd_h,
    mixed_o, tgrad_o, gg_o, gwg_o, gwu_o, gwd_o,
    gath, meta, mats, sel, rows, scal, wg, wu, wd, own, psend, precv, ret, rret,
    zs, zq, zrx, zqr, fin, finr, finq, finqr, hid, dgu, gwg, gwu, gwd,
    w_sem, zt_s, zt_r, pd_s, pd_r, cx_s, cx_r, px_s, px_r, pr_s, pr_r,
    zr_s, zr_r, zq_s, zq_r, f_s, f_r, o_sem,
):
    e = lax.axis_index("expert")
    h = lax.axis_index("half")
    x, z, y = e // (NZ * NY), (e // NY) % NZ, e % NY
    me = x * NY + y
    hs = pl.multiple_of(h * HALF, HALF)
    ho = pl.multiple_of((1 - h) * HALF, HALF)

    def at_z(dz):
        return ((x * NZ + (z + dz + NZ) % NZ) * NY + y, h)

    def in_plane(r):
        xx = (x + r // NY) % NX
        yy = (y + r % NY) % NY
        return ((xx * NZ + z) * NY + yy, h), xx * NY + yy

    partner = (e, 1 - h)

    loads = [
        pltpu.make_async_copy(src.at[0], dst, w_sem.at[i])
        for i, (src, dst) in enumerate(((wg_h, wg), (wu_h, wu), (wd_h, wd)))
    ]
    for c in loads:
        c.start()

    barrier = pltpu.get_barrier_semaphore()

    @pl.loop(1, PLANE)
    def _(r):
        pl.semaphore_signal(barrier, inc=1, device_id=in_plane(r)[0], device_id_type=MESH)

    @pl.loop(1, NZ)
    def _(r):
        pl.semaphore_signal(barrier, inc=1, device_id=at_z(r), device_id_type=MESH)

    pl.semaphore_signal(barrier, inc=1, device_id=partner, device_id_type=MESH)

    gath[z, 0:TOK, :] = tok[:, pl.ds(hs, HALF)]
    gath[z, TOK : 2 * TOK, :] = cot[:, pl.ds(hs, HALF)]
    meta[z] = jnp.zeros((TOK, 128), F32)
    meta[z, :, 0:TOP] = routes[...].astype(F32)
    meta[z, :, TOP : 2 * TOP] = gates[...]
    pl.semaphore_wait(barrier, PLANE - 1 + NZ - 1 + 1)

    def hop(stream, way, d, src_z):
        ref = meta.at[src_z] if stream == 2 else gath.at[src_z, pl.ds(stream * TOK, TOK)]
        return pltpu.make_async_remote_copy(
            src_ref=ref,
            dst_ref=ref,
            send_sem=zt_s.at[stream, way, d - 1],
            recv_sem=zt_r.at[stream, way, d - 1],
            device_id=at_z(1 if way == 0 else -1),
            device_id_type=MESH,
        )

    reach = ((4, 3), (3, 4), (4, 3))
    hops = []
    for way in (0, 1):
        for stream in (0, 1, 2):
            c = hop(stream, way, 1, z)
            c.start()
            hops.append(c)

    def arrive(d):
        for way in (0, 1):
            src = (z - d + NZ) % NZ if way == 0 else (z + d) % NZ
            for stream in (0, 1, 2):
                if d <= reach[stream][way]:
                    hop(stream, way, d, src).wait_recv()
                    if d + 1 <= reach[stream][way]:
                        c = hop(stream, way, d + 1, src)
                        c.start()
                        hops.append(c)

    lane = lax.broadcasted_iota(jnp.int32, (2 * TOK, ROWS), 1)
    row = lax.broadcasted_iota(jnp.int32, (2 * TOK, ROWS), 0)
    ids = ((lane // (NY * 2 * CAP)) * NZ + z) * NY + (lane // (2 * CAP)) % NY
    ids = jnp.where((lane // CAP) % 2 == row // TOK, ids, -1).astype(F32)
    place = (lane % CAP).astype(F32)

    def pair(s):
        a, b = OFFSETS[s]
        return (z + a + NZ) % NZ, (z + b + NZ) % NZ

    def both(ref, za, zb, lo, n):
        return jnp.concatenate([ref[za, lo : lo + n, :], ref[zb, lo : lo + n, :]], axis=0)

    def select(s):
        za, zb = pair(s)
        info = both(meta, za, zb, 0, TOK)
        named = jnp.zeros((2 * TOK, ROWS), F32)
        weight = jnp.zeros((2 * TOK, ROWS), F32)
        for k in range(TOP):
            hit = info[:, k : k + 1] == ids
            named = jnp.where(hit, 1.0, named)
            weight = jnp.where(hit, info[:, TOP + k : TOP + k + 1], weight)
        r0 = lax.broadcasted_iota(jnp.int32, (2 * TOK, 2 * TOK), 0)
        r1 = lax.broadcasted_iota(jnp.int32, (2 * TOK, 2 * TOK), 1)
        before = jnp.where(r1 < r0, 1.0, 0.0).astype(BF)
        placed = dot(before, named.astype(BF), 1, 0)
        one = jnp.where(placed == place, named, 0.0)
        weight = one * weight
        high = weight.astype(BF)
        low = (weight - high.astype(F32)).astype(BF)
        one = one.astype(BF)
        mats[s, 0 : 2 * TOK, :] = one
        mats[s, 2 * TOK : 4 * TOK, :] = high
        mats[s, 4 * TOK : 6 * TOK, :] = low
        tokens = both(gath, za, zb, 0, TOK)
        cots = both(gath, za, zb, TOK, TOK)
        sel[s, 0:ROWS, :] = dot(one, tokens, 0, 0).astype(BF)
        sel[s, ROWS : 2 * ROWS, :] = dot(
            jnp.concatenate([high, low], axis=0), jnp.concatenate([cots, cots], axis=0), 0, 0
        ).astype(BF)

    def block(p):
        return pl.ds(pl.multiple_of(p * 2 * CAP, 2 * CAP), 2 * CAP)

    def block_at(base, p):
        return pl.ds(pl.multiple_of(base + p * 2 * CAP, 2 * CAP), 2 * CAP)

    def dispatch(s):
        @pl.loop(1, PLANE)
        def _(r):
            dev, p = in_plane(r)
            for t, dst in ((0, rows), (1, scal)):
                pltpu.make_async_remote_copy(
                    src_ref=sel.at[s, block_at(t * ROWS, p)],
                    dst_ref=dst.at[block_at(s * ROWS, me), pl.ds(hs, HALF)],
                    send_sem=pd_s.at[s],
                    recv_sem=pd_r.at[s],
                    device_id=dev,
                    device_id_type=MESH,
                ).start()

        for t, dst in ((0, rows), (1, scal)):
            dst[block_at(s * ROWS, me), pl.ds(hs, HALF)] = sel[s, block_at(t * ROWS, me)]

    def bulk(sem):
        blocks = sel.at[0, pl.ds(0, 2 * ROWS - 4 * CAP)]
        return pltpu.make_async_copy(blocks, blocks, sem)

    arrive(1)
    select(0)
    dispatch(0)
    arrive(2)
    arrive(3)
    arrive(4)
    for s in range(1, STEPS):
        select(s)
        dispatch(s)

    for c in loads:
        c.wait()

    @pl.loop(0, STEPS)
    def _(s):
        at = pl.ds(pl.multiple_of(s * ROWS, ROWS), ROWS)
        bulk(pd_r.at[s]).wait()
        swaps = []
        for t, ref in ((0, rows), (1, scal)):
            c = pltpu.make_async_remote_copy(
                src_ref=ref.at[at, pl.ds(hs, HALF)],
                dst_ref=ref.at[at, pl.ds(hs, HALF)],
                send_sem=cx_s.at[s, t],
                recv_sem=cx_r.at[s, t],
                device_id=partner,
                device_id_type=MESH,
            )
            c.start()
            swaps.append(c)
        for c in swaps:
            c.wait()
        r = rows[at, :]
        pre_gate = dot(r, wg[...], 1, 0)
        pre_up = dot(r, wu[...], 1, 0)
        back = dot(scal[at, :], wd[...], 1, 1)
        sigma = jax.nn.sigmoid(pre_gate)
        hidden = (pre_gate * sigma * pre_up).astype(BF)
        d_up = (back * pre_gate * sigma).astype(BF)
        d_gate = (back * pre_up * sigma * (1.0 + pre_gate * (1.0 - sigma))).astype(BF)
        hid[at, :] = hidden
        dgu[at, 0:HID] = d_gate
        dgu[at, HID : 2 * HID] = d_up
        for base, dst in ((ho, None), (hs, own)):
            for q in range(2):
                f = pl.ds(pl.multiple_of(base + q * 512, 512), 512)
                g = dot(d_gate, wg[f, :], 1, 1) + dot(d_up, wu[f, :], 1, 1)
                o = dot(hidden, wd[:, f], 1, 0)
                if dst is None:
                    psend[s, 0:ROWS, q * 512 : (q + 1) * 512] = g.astype(BF)
                    psend[s, ROWS : 2 * ROWS, q * 512 : (q + 1) * 512] = o.astype(BF)
                else:
                    own[0:ROWS, q * 512 : (q + 1) * 512] = g
                    own[ROWS : 2 * ROWS, q * 512 : (q + 1) * 512] = o
            if dst is None:
                swap = pltpu.make_async_remote_copy(
                    src_ref=psend.at[s],
                    dst_ref=precv.at[s],
                    send_sem=px_s.at[s],
                    recv_sem=px_r.at[s],
                    device_id=partner,
                    device_id_type=MESH,
                )
                swap.start()
        swap.wait()
        ret[s] = (own[...] + precv[s].astype(F32)).astype(BF)

        @pl.loop(1, PLANE)
        def _(k):
            dev, p = in_plane(k)
            for t in (0, 1):
                pltpu.make_async_remote_copy(
                    src_ref=ret.at[s, block_at(t * ROWS, p)],
                    dst_ref=rret.at[s, block_at(t * ROWS, me)],
                    send_sem=pr_s.at[s],
                    recv_sem=pr_r.at[s],
                    device_id=dev,
                    device_id_type=MESH,
                ).start()

        for t in (0, 1):
            rret[s, block_at(t * ROWS, me), :] = ret[s, block_at(t * ROWS, me), :]

    @pl.loop(0, D // 256)
    def _(i):
        f = pl.ds(pl.multiple_of(i * 256, 256), 256)
        g = dot(rows[:, f], dgu[...], 0, 0)
        gwg[f, :] = g[:, 0:HID].astype(BF)
        gwu[f, :] = g[:, HID : 2 * HID].astype(BF)
        gwd[:, f] = dot(hid[...], scal[:, f], 0, 0).astype(BF)

    stores = [
        pltpu.make_async_copy(src, dst.at[0], o_sem.at[i])
        for i, (src, dst) in enumerate(((gwg, gwg_o), (gwu, gwu_o), (gwd, gwd_o)))
    ]
    for c in stores:
        c.start()

    sends = []
    lane128 = lax.broadcasted_iota(jnp.int32, (2 * TOK, 128), 1)
    for s in range(STEPS):
        za, zb = pair(s)
        bulk(pr_r.at[s]).wait()
        g = rret[s, 0:ROWS, :]
        o = rret[s, ROWS : 2 * ROWS, :]
        one = mats[s, 0 : 2 * TOK, :]
        tg = dot(one, g, 1, 0)
        mx = dot(mats[s, 2 * TOK : 4 * TOK, :], o, 1, 0) + dot(mats[s, 4 * TOK : 6 * TOK, :], o, 1, 0)
        inner = dot(both(gath, za, zb, TOK, TOK), o, 1, 1) * one.astype(F32)
        info = both(meta, za, zb, 0, TOK)
        quot = jnp.zeros((2 * TOK, 128), F32)
        for k in range(TOP):
            hit = info[:, k : k + 1] == ids
            v = jnp.sum(jnp.where(hit, inner, 0.0), axis=1, keepdims=True)
            quot = jnp.where(lane128 == k, v, quot)
        for i, zz in ((0, za), (1, zb)):
            part = slice(i * TOK, (i + 1) * TOK)
            if OFFSETS[s][i] == 0:
                zrx[z, 0:TOK, :] = mx[part, :].astype(BF)
                zrx[z, TOK : 2 * TOK, :] = tg[part, :].astype(BF)
                zqr[z] = quot[part, :]
                continue
            zs[s, i, 0:TOK, :] = mx[part, :].astype(BF)
            zs[s, i, TOK : 2 * TOK, :] = tg[part, :].astype(BF)
            zq[s, i] = quot[part, :]
            for src, dst, ss, rs in ((zs, zrx, zr_s, zr_r), (zq, zqr, zq_s, zq_r)):
                c = pltpu.make_async_remote_copy(
                    src_ref=src.at[s, i],
                    dst_ref=dst.at[z],
                    send_sem=ss.at[s, i],
                    recv_sem=rs.at[z],
                    device_id=at_z(OFFSETS[s][i]),
                    device_id_type=MESH,
                )
                c.start()
                sends.append(c)

    @pl.loop(1, NZ)
    def _(r):
        zz = (z + r) % NZ
        pltpu.make_async_copy(zrx.at[zz], zrx.at[zz], zr_r.at[zz]).wait()
        pltpu.make_async_copy(zqr.at[zz], zqr.at[zz], zq_r.at[zz]).wait()

    total = zrx[0].astype(F32)
    quot = zqr[0]
    for i in range(1, NZ):
        total += zrx[i].astype(F32)
        quot += zqr[i]
    fin[...] = total.astype(BF)
    finq[...] = quot
    last = [
        pltpu.make_async_remote_copy(
            src_ref=src, dst_ref=dst, send_sem=f_s.at[i], recv_sem=f_r.at[i],
            device_id=partner, device_id_type=MESH,
        )
        for i, (src, dst) in enumerate(((fin, finr), (finq, finqr)))
    ]
    for c in last:
        c.start()
    mixed_o[:, pl.ds(hs, HALF)] = fin[0:TOK, :]
    tgrad_o[:, pl.ds(hs, HALF)] = fin[TOK : 2 * TOK, :]
    for c in last:
        c.wait()
    mixed_o[:, pl.ds(ho, HALF)] = finr[0:TOK, :]
    tgrad_o[:, pl.ds(ho, HALF)] = finr[TOK : 2 * TOK, :]
    gg_o[...] = (quot + finqr[...])[:, 0:TOP]

    for c in hops:
        c.wait_send()
    for s in range(STEPS):
        bulk(pd_s.at[s]).wait()
        bulk(pr_s.at[s]).wait()
    for c in sends:
        c.wait_send()
    for c in stores:
        c.wait()


def body(tokens, routes, gates, cotangent, w_gate, w_up, w_down):
    vm = pl.BlockSpec(memory_space=pltpu.VMEM)
    hbm = pl.BlockSpec(memory_space=pl.ANY)
    dma = pltpu.SemaphoreType.DMA
    return pl.pallas_call(
        kernel,
        out_shape=(
            jax.ShapeDtypeStruct((TOK, D), BF),
            jax.ShapeDtypeStruct((TOK, D), BF),
            jax.ShapeDtypeStruct((TOK, TOP), F32),
            jax.ShapeDtypeStruct((1, D, HID), BF),
            jax.ShapeDtypeStruct((1, D, HID), BF),
            jax.ShapeDtypeStruct((1, HID, D), BF),
        ),
        in_specs=[vm] * 4 + [hbm] * 3,
        out_specs=(vm, vm, vm, hbm, hbm, hbm),
        scratch_shapes=[
            pltpu.VMEM((NZ, 2 * TOK, HALF), BF),
            pltpu.VMEM((NZ, TOK, 128), F32),
            pltpu.VMEM((STEPS, 6 * TOK, ROWS), BF),
            pltpu.VMEM((STEPS, 2 * ROWS, HALF), BF),
            pltpu.VMEM((STEPS * ROWS, D), BF),
            pltpu.VMEM((STEPS * ROWS, D), BF),
            pltpu.VMEM((D, HID), BF),
            pltpu.VMEM((D, HID), BF),
            pltpu.VMEM((HID, D), BF),
            pltpu.VMEM((2 * ROWS, HALF), F32),
            pltpu.VMEM((STEPS, 2 * ROWS, HALF), BF),
            pltpu.VMEM((STEPS, 2 * ROWS, HALF), BF),
            pltpu.VMEM((STEPS, 2 * ROWS, HALF), BF),
            pltpu.VMEM((STEPS, 2 * ROWS, HALF), BF),
            pltpu.VMEM((STEPS, 2, 2 * TOK, HALF), BF),
            pltpu.VMEM((STEPS, 2, TOK, 128), F32),
            pltpu.VMEM((NZ, 2 * TOK, HALF), BF),
            pltpu.VMEM((NZ, TOK, 128), F32),
            pltpu.VMEM((2 * TOK, HALF), BF),
            pltpu.VMEM((2 * TOK, HALF), BF),
            pltpu.VMEM((TOK, 128), F32),
            pltpu.VMEM((TOK, 128), F32),
            pltpu.VMEM((STEPS * ROWS, HID), BF),
            pltpu.VMEM((STEPS * ROWS, 2 * HID), BF),
            pltpu.VMEM((D, HID), BF),
            pltpu.VMEM((D, HID), BF),
            pltpu.VMEM((HID, D), BF),
            dma((3,)),
            dma((3, 2, 4)),
            dma((3, 2, 4)),
            dma((STEPS,)),
            dma((STEPS,)),
            dma((STEPS, 2)),
            dma((STEPS, 2)),
            dma((STEPS,)),
            dma((STEPS,)),
            dma((STEPS,)),
            dma((STEPS,)),
            dma((STEPS, 2)),
            dma((NZ,)),
            dma((STEPS, 2)),
            dma((NZ,)),
            dma((2,)),
            dma((2,)),
            dma((3,)),
        ],
        compiler_params=pltpu.CompilerParams(
            collective_id=0, has_side_effects=True, vmem_limit_bytes=60 << 20
        ),
        name="moe",
    )(tokens, cotangent, routes, gates, w_gate, w_up, w_down)


def solution(mesh):
    placed = (
        P("expert", None),
        P("expert", None),
        P("expert", None),
        P("expert", None),
        P("expert", None, "half"),
        P("expert", None, "half"),
        P("expert", "half", None),
    )
    return jax.shard_map(
        body,
        mesh=mesh,
        in_specs=placed,
        out_specs=(
            P("expert", None),
            P("expert", None),
            P("expert", None),
            P("expert", None, "half"),
            P("expert", None, "half"),
            P("expert", "half", None),
        ),
        check_vma=False,
    )
```

```python
import jax
import jax.numpy as jnp
from jax import lax
from jax.experimental import pallas as pl
from jax.experimental.pallas import tpu as pltpu
from jax.sharding import PartitionSpec as P

MESH = pl.DeviceIdType.MESH
NX, NZ, NY = 4, 8, 4
PLANE = NX * NY
TOK = 64
D = 2048
HALF = D // 2
HID = 384
TOP = 8
CAP = 8
ROWS = PLANE * 2 * CAP
FAR_FIRST = (10, 6, 9, 11, 14, 5, 7, 13, 15, 2, 8, 1, 4, 3, 12)
BF = jnp.bfloat16
F32 = jnp.float32


def dot(a, b, ca, cb):
    return lax.dot_general(a, b, (((ca,), (cb,)), ((), ())), preferred_element_type=F32)


def kernel(
    tok, cot, routes, gates, wg_h, wu_h, wd_h,
    mixed_o, tgrad_o, gg_o, gwg_o, gwu_o, gwd_o,
    gath, meta, mats, sel, recv, wg, wu, wd, own, psend, precv, ret, rret,
    zs, zq, zx, zqx, fin, finr, finq, finqr, hid, dgu, gwg, gwu, gwd,
    w_sem, zt_s, zt_r, pd_s, pd_r, cx_s, cx_r, px_s, px_r, pr_s, pr_r,
    zr_s, zr_r, zq_s, zq_r, f_s, f_r, o_sem,
):
    e = lax.axis_index("expert")
    h = lax.axis_index("half")
    x, z, y = e // (NZ * NY), (e // NY) % NZ, e % NY
    me = x * NY + y
    mine = pl.ds(pl.multiple_of(h * HALF, HALF), HALF)
    other = pl.ds(pl.multiple_of((1 - h) * HALF, HALF), HALF)

    def at_z(dz):
        return ((x * NZ + (z + dz) % NZ) * NY + y, h)

    def in_plane(r):
        xx = (x + r // NY) % NX
        yy = (y + r % NY) % NY
        return ((xx * NZ + z) * NY + yy, h), xx * NY + yy

    partner = (e, 1 - h)

    def remote(src, dst, ss, rs, dev):
        return pltpu.make_async_remote_copy(
            src_ref=src, dst_ref=dst, send_sem=ss, recv_sem=rs, device_id=dev, device_id_type=MESH
        )

    loads = [
        pltpu.make_async_copy(src.at[0], dst, w_sem.at[i])
        for i, (src, dst) in enumerate(((wg_h, wg), (wu_h, wu), (wd_h, wd)))
    ]
    for c in loads:
        c.start()

    barrier = pltpu.get_barrier_semaphore()
    for r in range(1, PLANE):
        pl.semaphore_signal(barrier, inc=1, device_id=in_plane(r)[0], device_id_type=MESH)
    for r in range(1, NZ):
        pl.semaphore_signal(barrier, inc=1, device_id=at_z(r), device_id_type=MESH)
    pl.semaphore_signal(barrier, inc=1, device_id=partner, device_id_type=MESH)

    gath[z, 0:TOK, :] = tok[:, mine]
    gath[z, TOK : 2 * TOK, :] = cot[:, mine]
    flat = jnp.concatenate([routes[...].astype(F32), gates[...]], axis=0)
    flat = jnp.concatenate([flat, jnp.zeros((112, TOK), F32)], axis=0)
    meta[z] = flat.T

    lane = lax.broadcasted_iota(jnp.int32, (TOK, ROWS), 1)
    expert = lane // (2 * CAP)
    ids = ((expert // NY * NZ + z) * NY + expert % NY).astype(F32)
    slot = (lane % CAP).astype(F32)
    kind = ((lane // CAP) % 2).astype(F32)

    def select(s):
        zz = (z + s) % NZ
        info = meta[zz]
        named = jnp.zeros((TOK, ROWS), F32)
        weight = jnp.zeros((TOK, ROWS), F32)
        for k in range(TOP):
            hit = info[:, k : k + 1] == ids
            named = jnp.where(hit, 1.0, named)
            weight = jnp.where(hit, info[:, TOP + k : TOP + k + 1], weight)
        r0 = lax.broadcasted_iota(jnp.int32, (TOK, TOK), 0)
        r1 = lax.broadcasted_iota(jnp.int32, (TOK, TOK), 1)
        before = jnp.where(r1 < r0, 1.0, 0.0).astype(BF)
        placed = dot(before, named.astype(BF), 1, 0)
        one = jnp.where(placed == slot, named, 0.0)
        out_one = one * kind
        weight = out_one * weight
        high = weight.astype(BF)
        low = (weight - high.astype(F32)).astype(BF)
        mats[s, 0:TOK, :] = (one - out_one).astype(BF)
        mats[s, TOK : 2 * TOK, :] = high
        mats[s, 2 * TOK : 3 * TOK, :] = low
        mats[s, 3 * TOK : 4 * TOK, :] = out_one.astype(BF)
        source = jnp.concatenate([gath[zz], gath[zz, TOK : 2 * TOK, :]], axis=0)
        sel[s] = dot(mats[s, 0 : 3 * TOK, :], source, 0, 0).astype(BF)

    select(0)
    pl.semaphore_wait(barrier, PLANE - 1 + NZ - 1 + 1)

    def hop(stream, way, d, src_z):
        ref = meta.at[src_z] if stream == 2 else gath.at[src_z, pl.ds(stream * TOK, TOK)]
        return remote(
            ref, ref, zt_s.at[stream, way, d - 1], zt_r.at[stream, way, d - 1],
            at_z(1 if way == 0 else NZ - 1),
        )

    reach = ((4, 3), (3, 4), (4, 3))
    hops = []
    for stream in (2, 0, 1):
        for way in (1, 0):
            c = hop(stream, way, 1, z)
            c.start()
            hops.append(c)

    def arrive(d):
        for stream in (2, 0, 1):
            for way in (1, 0):
                if d <= reach[stream][way]:
                    src = (z + NZ - d) % NZ if way == 0 else (z + d) % NZ
                    hop(stream, way, d, src).wait_recv()
                    if d + 1 <= reach[stream][way]:
                        c = hop(stream, way, d + 1, src)
                        c.start()
                        hops.append(c)

    def block(p):
        return pl.ds(pl.multiple_of(p * 2 * CAP, 2 * CAP), 2 * CAP)

    def dispatch(s):
        for r in FAR_FIRST:
            dev, p = in_plane(r)
            remote(
                sel.at[s, block(p)], recv.at[s, block(me), mine], pd_s.at[s], pd_r.at[s], dev
            ).start()
        recv[s, block(me), mine] = sel[s, block(me), :]

    def bulk(sem):
        blocks = sel.at[0, pl.ds(0, ROWS - 2 * CAP)]
        pltpu.make_async_copy(blocks, blocks, sem).wait()

    dispatch(0)
    for s in range(1, NZ):
        if s <= 4:
            arrive(s)
        select(s)
        dispatch(s)

    for c in loads:
        c.wait()

    def exchange(s):
        return remote(
            recv.at[s, :, mine], recv.at[s, :, mine], cx_s.at[s], cx_r.at[s], partner
        )

    def partial(s):
        return remote(psend.at[s % 2], precv.at[s % 4], px_s.at[s], px_r.at[s], partner)

    half = ROWS // 2

    def expert_step(s):
        at = pl.ds(pl.multiple_of(s * half, half), half)
        for q in range(4):
            f = slice(q * 512, (q + 1) * 512)
            v = recv[s, :, f].astype(F32).reshape(PLANE, 2, CAP, 512)
            recv[s, 0:half, f] = v[:, 0].reshape(half, 512).astype(BF)
            recv[s, half:ROWS, f] = v[:, 1].reshape(half, 512).astype(BF)
        r = recv[s, 0:half, :]
        pre_gate = dot(r, wg[...], 1, 0)
        pre_up = dot(r, wu[...], 1, 0)
        back = dot(recv[s, half:ROWS, :], wd[...], 1, 1)
        sigma = jax.nn.sigmoid(pre_gate)
        hidden = (pre_gate * sigma * pre_up).astype(BF)
        d_up = (back * pre_gate * sigma).astype(BF)
        d_gate = (back * pre_up * sigma * (1.0 + pre_gate * (1.0 - sigma))).astype(BF)
        hid[at, :] = hidden
        dgu[at, 0:HID] = d_gate
        dgu[at, HID : 2 * HID] = d_up
        p = s % 2
        psend[p, 0:half, :] = (dot(d_gate, wg[other, :], 1, 1) + dot(d_up, wu[other, :], 1, 1)).astype(BF)
        psend[p, half:ROWS, :] = dot(hidden, wd[:, other], 1, 0).astype(BF)
        partial(s).start()
        own[p, 0:half, :] = dot(d_gate, wg[mine, :], 1, 1) + dot(d_up, wu[mine, :], 1, 1)
        own[p, half:ROWS, :] = dot(hidden, wd[:, mine], 1, 0)

    def go_home(s):
        partial(s).wait()
        v = own[s % 2] + precv[s % 4].astype(F32)
        v = jnp.concatenate(
            [v[0:half].reshape(PLANE, 1, CAP, HALF), v[half:ROWS].reshape(PLANE, 1, CAP, HALF)], axis=1
        )
        ret[s] = v.reshape(ROWS, HALF).astype(BF)
        for k in FAR_FIRST:
            dev, p = in_plane(k)
            remote(ret.at[s, block(p)], rret.at[s, block(me)], pr_s.at[s], pr_r.at[s], dev).start()
        rret[s, block(me), :] = ret[s, block(me), :]

    lane128 = lax.broadcasted_iota(jnp.int32, (TOK, 128), 1)

    def leave(s):
        dz = s + (s // 4) * (NZ - 1 - s)
        return remote(zs.at[s], zx.at[s], zr_s.at[s], zr_r.at[s], at_z(dz))

    def leave_inner(s):
        return remote(zq.at[s], zqx.at[s], zq_s.at[s], zq_r.at[s], at_z(s))

    def gather_home(s, chained=False):
        zz = (z + s) % NZ
        bulk(pr_r.at[s])
        r = rret[s]
        sums = dot(mats[s, 0 : 3 * TOK, :], r, 1, 0)
        mx = sums[TOK : 2 * TOK] + sums[2 * TOK : 3 * TOK]
        tg = sums[0:TOK]
        inner = dot(gath[zz, TOK : 2 * TOK, :], r, 1, 1) * mats[s, 3 * TOK : 4 * TOK, :].astype(F32)
        if chained:
            leave(s - 1).wait_recv()
            mx += zx[s - 1, 0:TOK, :].astype(F32)
            tg += zx[s - 1, TOK : 2 * TOK, :].astype(F32)
        zs[s, 0:TOK, :] = mx.astype(BF)
        zs[s, TOK : 2 * TOK, :] = tg.astype(BF)

        @pl.when(s > 0)
        def _():
            leave(s).start()

        info = meta[zz]
        quot = jnp.zeros((TOK, 128), F32)
        for k in range(TOP):
            hit = info[:, k : k + 1] == ids
            v = jnp.sum(jnp.where(hit, inner, 0.0), axis=1, keepdims=True)
            quot = jnp.where(lane128 == k, v, quot)
        zq[s] = jnp.concatenate([quot, jnp.zeros((128 - TOK, 128), F32)], axis=0).T[0:TOP, :]

        @pl.when(s > 0)
        def _():
            leave_inner(s).start()

    bulk(pd_r.at[0])
    exchange(0).start()

    @pl.loop(0, NZ)
    def _(s):
        @pl.when(s < NZ - 1)
        def _():
            bulk(pd_r.at[s + 1])
            exchange(s + 1).start()

        exchange(s).wait()
        expert_step(s)

        @pl.when(s > 0)
        def _():
            go_home(s - 1)

        @pl.when(s > 2)
        def _():
            gather_home(s - 3)

    go_home(NZ - 1)

    def weights(i):
        f = pl.ds(pl.multiple_of(i * 256, 256), 256)
        g = dot(recv[:, 0:half, f].reshape(NZ * half, 256), dgu[...], 0, 0)
        gwg[f, :] = g[:, 0:HID].astype(BF)
        gwu[f, :] = g[:, HID : 2 * HID].astype(BF)
        gwd[:, f] = dot(hid[...], recv[:, half:ROWS, f].reshape(NZ * half, 256), 0, 0).astype(BF)

    pl.loop(0, 4)(weights)
    gather_home(NZ - 3, chained=True)
    pl.loop(4, D // 256)(weights)
    stores = [
        pltpu.make_async_copy(src, dst.at[0], o_sem.at[i])
        for i, (src, dst) in enumerate(((gwg, gwg_o), (gwu, gwu_o), (gwd, gwd_o)))
    ]
    for c in stores:
        c.start()
    gather_home(NZ - 2, chained=True)
    gather_home(NZ - 1, chained=True)

    total = zs[0].astype(F32)
    quot = zq[0]
    for s in range(1, NZ):
        leave_inner(s).wait_recv()
        quot += zqx[s]
    for s in (1, 2, 3, NZ - 1):
        leave(s).wait_recv()
        total += zx[s].astype(F32)
    fin[...] = total.astype(BF)
    finq[...] = quot
    last = [
        remote(src, dst, f_s.at[i], f_r.at[i], partner)
        for i, (src, dst) in enumerate(((fin, finr), (finq, finqr)))
    ]
    for c in last:
        c.start()
    mixed_o[:, mine] = fin[0:TOK, :]
    tgrad_o[:, mine] = fin[TOK : 2 * TOK, :]
    for c in last:
        c.wait()
    mixed_o[:, other] = finr[0:TOK, :]
    tgrad_o[:, other] = finr[TOK : 2 * TOK, :]
    gg_o[...] = (quot + finqr[...])[:, 0:TOK]

    for c in hops:
        c.wait_send()
    for s in range(NZ):
        bulk(pd_s.at[s])
        bulk(pr_s.at[s])
        if s:
            leave(s).wait_send()
            leave_inner(s).wait_send()
    for c in stores:
        c.wait()


def place(*refs):
    src, dst, held, (sem_in, sem_out) = refs[0:6], refs[6:12], refs[12:18], refs[18:20]
    into = [pltpu.make_async_copy(src[i], held[i], sem_in.at[i]) for i in range(6)]
    out = [pltpu.make_async_copy(held[i], dst[i], sem_out.at[i]) for i in range(6)]
    for c in into:
        c.start()
    for a, b in zip(into, out):
        a.wait()
        b.start()
    for b in out:
        b.wait()


def body(tokens, routes, gates, cotangent, w_gate, w_up, w_down):
    vm = pl.BlockSpec(memory_space=pltpu.VMEM)
    hbm = pl.BlockSpec(memory_space=pl.ANY)
    dma = pltpu.SemaphoreType.DMA
    shapes = (
        jax.ShapeDtypeStruct((TOK, D), BF),
        jax.ShapeDtypeStruct((TOK, D), BF),
        jax.ShapeDtypeStruct((TOP, TOK), F32),
        jax.ShapeDtypeStruct((1, D, HID), BF),
        jax.ShapeDtypeStruct((1, D, HID), BF),
        jax.ShapeDtypeStruct((1, HID, D), BF),
    )
    outs = pl.pallas_call(
        kernel,
        out_shape=shapes,
        in_specs=[vm] * 4 + [hbm] * 3,
        out_specs=(vm, vm, vm, hbm, hbm, hbm),
        scratch_shapes=[
            pltpu.VMEM((NZ, 2 * TOK, HALF), BF),
            pltpu.VMEM((NZ, TOK, 128), F32),
            pltpu.VMEM((NZ, 4 * TOK, ROWS), BF),
            pltpu.VMEM((NZ, ROWS, HALF), BF),
            pltpu.VMEM((NZ, ROWS, D), BF),
            pltpu.VMEM((D, HID), BF),
            pltpu.VMEM((D, HID), BF),
            pltpu.VMEM((HID, D), BF),
            pltpu.VMEM((2, ROWS, HALF), F32),
            pltpu.VMEM((2, ROWS, HALF), BF),
            pltpu.VMEM((4, ROWS, HALF), BF),
            pltpu.VMEM((NZ, ROWS, HALF), BF),
            pltpu.VMEM((NZ, ROWS, HALF), BF),
            pltpu.VMEM((NZ, 2 * TOK, HALF), BF),
            pltpu.VMEM((NZ, TOP, 128), F32),
            pltpu.VMEM((NZ, 2 * TOK, HALF), BF),
            pltpu.VMEM((NZ, TOP, 128), F32),
            pltpu.VMEM((2 * TOK, HALF), BF),
            pltpu.VMEM((2 * TOK, HALF), BF),
            pltpu.VMEM((TOP, 128), F32),
            pltpu.VMEM((TOP, 128), F32),
            pltpu.VMEM((NZ * ROWS // 2, HID), BF),
            pltpu.VMEM((NZ * ROWS // 2, 2 * HID), BF),
            pltpu.VMEM((D, HID), BF),
            pltpu.VMEM((D, HID), BF),
            pltpu.VMEM((HID, D), BF),
            dma((3,)),
            dma((3, 2, 4)),
            dma((3, 2, 4)),
        ]
        + [dma((NZ,))] * 12
        + [dma((2,)), dma((2,)), dma((3,))],
        compiler_params=pltpu.CompilerParams(
            collective_id=0, has_side_effects=True, vmem_limit_bytes=60 << 20
        ),
        name="moe",
    )(tokens, cotangent, routes.T, gates.T, w_gate, w_up, w_down)
    outs = pl.pallas_call(
        place,
        out_shape=shapes,
        in_specs=[hbm] * 6,
        out_specs=[hbm] * 6,
        scratch_shapes=[pltpu.VMEM(o.shape, o.dtype) for o in shapes] + [dma((6,)), dma((6,))],
        compiler_params=pltpu.CompilerParams(vmem_limit_bytes=60 << 20),
        name="place",
    )(*outs)
    return (outs[0], outs[1], outs[2].T) + tuple(outs[3:])


def solution(mesh):
    placed = (
        P("expert", None),
        P("expert", None),
        P("expert", None),
        P("expert", None),
        P("expert", None, "half"),
        P("expert", None, "half"),
        P("expert", "half", None),
    )
    return jax.shard_map(
        body,
        mesh=mesh,
        in_specs=placed,
        out_specs=(
            P("expert", None),
            P("expert", None),
            P("expert", None),
            P("expert", None, "half"),
            P("expert", None, "half"),
            P("expert", "half", None),
        ),
        check_vma=False,
    )
```

```python
import jax
import jax.numpy as jnp
from jax import lax
from jax.experimental import pallas as pl
from jax.experimental.pallas import tpu as pltpu
from jax.sharding import PartitionSpec as P

MESH = pl.DeviceIdType.MESH
NX, NZ, NY = 4, 8, 4
PLANE = NX * NY
TOK = 64
D = 2048
HALF = D // 2
HID = 384
TOP = 8
CAP = 8
ROWS = PLANE * 2 * CAP
FAR_FIRST = (10, 6, 9, 11, 14, 5, 7, 13, 15, 2, 8, 1, 4, 3, 12)
BF = jnp.bfloat16
F32 = jnp.float32


def dot(a, b, ca, cb):
    return lax.dot_general(a, b, (((ca,), (cb,)), ((), ())), preferred_element_type=F32)


def kernel(
    tok, cot, routes, gates, wg_h, wu_h, wd_h,
    mixed_o, tgrad_o, gg_o, gwg_o, gwu_o, gwd_o,
    routes_v, gates_v, gath, meta, mats, sel, recv, wg, wu, wd, own, psend, precv, ret, rret,
    zs, zq, zx, zqx, fin, finr, finq, finqr, hid, dgu, gwg, gwu, gwd,
    i_sem, w_sem, zt_s, zt_r, pd_s, pd_r, cx_s, cx_r, px_s, px_r, pr_s, pr_r,
    zr_s, zr_r, zq_s, zq_r, f_s, f_r, o_sem,
):
    e = lax.axis_index("expert")
    h = lax.axis_index("half")
    x, z, y = e // (NZ * NY), (e // NY) % NZ, e % NY
    me = x * NY + y
    mine = pl.ds(pl.multiple_of(h * HALF, HALF), HALF)
    other = pl.ds(pl.multiple_of((1 - h) * HALF, HALF), HALF)

    def at_z(dz):
        return ((x * NZ + (z + dz) % NZ) * NY + y, h)

    def in_plane(r):
        xx = (x + r // NY) % NX
        yy = (y + r % NY) % NY
        return ((xx * NZ + z) * NY + yy, h), xx * NY + yy

    partner = (e, 1 - h)

    def remote(src, dst, ss, rs, dev):
        return pltpu.make_async_remote_copy(
            src_ref=src, dst_ref=dst, send_sem=ss, recv_sem=rs, device_id=dev, device_id_type=MESH
        )

    firsts = [
        pltpu.make_async_copy(tok.at[:, mine], gath.at[z, pl.ds(0, TOK)], i_sem.at[0]),
        pltpu.make_async_copy(cot.at[:, mine], gath.at[z, pl.ds(TOK, TOK)], i_sem.at[1]),
        pltpu.make_async_copy(routes, routes_v, i_sem.at[2]),
        pltpu.make_async_copy(gates, gates_v, i_sem.at[3]),
    ]
    for c in firsts:
        c.start()
    loads = [
        pltpu.make_async_copy(src.at[0], dst, w_sem.at[i])
        for i, (src, dst) in enumerate(((wg_h, wg), (wu_h, wu), (wd_h, wd)))
    ]
    for c in loads:
        c.start()

    barrier = pltpu.get_barrier_semaphore()
    for r in range(1, PLANE):
        pl.semaphore_signal(barrier, inc=1, device_id=in_plane(r)[0], device_id_type=MESH)
    for r in range(1, NZ):
        pl.semaphore_signal(barrier, inc=1, device_id=at_z(r), device_id_type=MESH)
    pl.semaphore_signal(barrier, inc=1, device_id=partner, device_id_type=MESH)

    for c in firsts:
        c.wait()
    flat = jnp.concatenate([routes_v[...].astype(F32), gates_v[...]], axis=0)
    flat = jnp.concatenate([flat, jnp.zeros((112, TOK), F32)], axis=0)
    meta[z] = flat.T

    lane = lax.broadcasted_iota(jnp.int32, (TOK, ROWS), 1)
    expert = lane // (2 * CAP)
    ids = ((expert // NY * NZ + z) * NY + expert % NY).astype(F32)
    slot = (lane % CAP).astype(F32)
    kind = ((lane // CAP) % 2).astype(F32)

    def select(s):
        zz = (z + s) % NZ
        info = meta[zz]
        named = jnp.zeros((TOK, ROWS), F32)
        weight = jnp.zeros((TOK, ROWS), F32)
        for k in range(TOP):
            hit = info[:, k : k + 1] == ids
            named = jnp.where(hit, 1.0, named)
            weight = jnp.where(hit, info[:, TOP + k : TOP + k + 1], weight)
        r0 = lax.broadcasted_iota(jnp.int32, (TOK, TOK), 0)
        r1 = lax.broadcasted_iota(jnp.int32, (TOK, TOK), 1)
        before = jnp.where(r1 < r0, 1.0, 0.0).astype(BF)
        placed = dot(before, named.astype(BF), 1, 0)
        one = jnp.where(placed == slot, named, 0.0)
        out_one = one * kind
        weight = out_one * weight
        high = weight.astype(BF)
        low = (weight - high.astype(F32)).astype(BF)
        mats[s, 0:TOK, :] = (one - out_one).astype(BF)
        mats[s, TOK : 2 * TOK, :] = high
        mats[s, 2 * TOK : 3 * TOK, :] = low
        mats[s, 3 * TOK : 4 * TOK, :] = out_one.astype(BF)
        source = jnp.concatenate([gath[zz], gath[zz, TOK : 2 * TOK, :]], axis=0)
        sel[s] = dot(mats[s, 0 : 3 * TOK, :], source, 0, 0).astype(BF)

    select(0)
    pl.semaphore_wait(barrier, PLANE - 1 + NZ - 1 + 1)

    def hop(stream, way, d, src_z):
        ref = meta.at[src_z] if stream == 2 else gath.at[src_z, pl.ds(stream * TOK, TOK)]
        return remote(
            ref, ref, zt_s.at[stream, way, d - 1], zt_r.at[stream, way, d - 1],
            at_z(1 if way == 0 else NZ - 1),
        )

    reach = ((4, 3), (3, 4), (4, 3))
    hops = []
    for stream in (2, 0, 1):
        for way in (1, 0):
            c = hop(stream, way, 1, z)
            c.start()
            hops.append(c)

    def arrive(d):
        for stream in (2, 0, 1):
            for way in (1, 0):
                if d <= reach[stream][way]:
                    src = (z + NZ - d) % NZ if way == 0 else (z + d) % NZ
                    hop(stream, way, d, src).wait_recv()
                    if d + 1 <= reach[stream][way]:
                        c = hop(stream, way, d + 1, src)
                        c.start()
                        hops.append(c)

    def block(p):
        return pl.ds(pl.multiple_of(p * 2 * CAP, 2 * CAP), 2 * CAP)

    def dispatch(s):
        for r in FAR_FIRST:
            dev, p = in_plane(r)
            remote(
                sel.at[s, block(p)], recv.at[s, block(me), mine], pd_s.at[s], pd_r.at[s], dev
            ).start()
        recv[s, block(me), mine] = sel[s, block(me), :]

    def bulk(sem):
        blocks = sel.at[0, pl.ds(0, ROWS - 2 * CAP)]
        pltpu.make_async_copy(blocks, blocks, sem).wait()

    dispatch(0)
    for s in range(1, NZ):
        if s <= 4:
            arrive(s)
        select(s)
        dispatch(s)

    for c in loads:
        c.wait()

    def exchange(s):
        return remote(
            recv.at[s, :, mine], recv.at[s, :, mine], cx_s.at[s], cx_r.at[s], partner
        )

    def turn(i):
        return (i + 1) % NZ

    def partial(i):
        return remote(psend.at[i % 2], precv.at[i % 4], px_s.at[i], px_r.at[i], partner)

    half = ROWS // 2

    def expert_step(i):
        s = turn(i)
        at = pl.ds(pl.multiple_of(s * half, half), half)
        for q in range(4):
            f = slice(q * 512, (q + 1) * 512)
            v = recv[s, :, f].astype(F32).reshape(PLANE, 2, CAP, 512)
            recv[s, 0:half, f] = v[:, 0].reshape(half, 512).astype(BF)
            recv[s, half:ROWS, f] = v[:, 1].reshape(half, 512).astype(BF)
        r = recv[s, 0:half, :]
        pre_gate = dot(r, wg[...], 1, 0)
        pre_up = dot(r, wu[...], 1, 0)
        back = dot(recv[s, half:ROWS, :], wd[...], 1, 1)
        sigma = jax.nn.sigmoid(pre_gate)
        hidden = (pre_gate * sigma * pre_up).astype(BF)
        d_up = (back * pre_gate * sigma).astype(BF)
        d_gate = (back * pre_up * sigma * (1.0 + pre_gate * (1.0 - sigma))).astype(BF)
        hid[at, :] = hidden
        dgu[at, 0:HID] = d_gate
        dgu[at, HID : 2 * HID] = d_up
        p = i % 2
        psend[p, 0:half, :] = (dot(d_gate, wg[other, :], 1, 1) + dot(d_up, wu[other, :], 1, 1)).astype(BF)
        psend[p, half:ROWS, :] = dot(hidden, wd[:, other], 1, 0).astype(BF)
        partial(i).start()
        own[p, 0:half, :] = dot(d_gate, wg[mine, :], 1, 1) + dot(d_up, wu[mine, :], 1, 1)
        own[p, half:ROWS, :] = dot(hidden, wd[:, mine], 1, 0)

    def go_home(i):
        s = turn(i)
        partial(i).wait()
        v = own[i % 2] + precv[i % 4].astype(F32)
        v = jnp.concatenate(
            [v[0:half].reshape(PLANE, 1, CAP, HALF), v[half:ROWS].reshape(PLANE, 1, CAP, HALF)], axis=1
        )
        ret[s] = v.reshape(ROWS, HALF).astype(BF)
        for k in FAR_FIRST:
            dev, p = in_plane(k)
            remote(ret.at[s, block(p)], rret.at[s, block(me)], pr_s.at[s], pr_r.at[s], dev).start()
        rret[s, block(me), :] = ret[s, block(me), :]

    lane128 = lax.broadcasted_iota(jnp.int32, (TOK, 128), 1)

    def leave(s):
        dz = s + (s // 4) * (NZ - 1 - s)
        return remote(zs.at[s], zx.at[s], zr_s.at[s], zr_r.at[s], at_z(dz))

    def leave_inner(s):
        return remote(zq.at[s], zqx.at[s], zq_s.at[s], zq_r.at[s], at_z(s))

    def sums_of(s):
        sums = dot(mats[s, 0 : 3 * TOK, :], rret[s], 1, 0)
        return sums[TOK : 2 * TOK] + sums[2 * TOK : 3 * TOK], sums[0:TOK]

    def inner_of(s):
        zz = (z + s) % NZ
        inner = dot(gath[zz, TOK : 2 * TOK, :], rret[s], 1, 1)
        inner = inner * mats[s, 3 * TOK : 4 * TOK, :].astype(F32)
        info = meta[zz]
        quot = jnp.zeros((TOK, 128), F32)
        for k in range(TOP):
            hit = info[:, k : k + 1] == ids
            v = jnp.sum(jnp.where(hit, inner, 0.0), axis=1, keepdims=True)
            quot = jnp.where(lane128 == k, v, quot)
        return jnp.concatenate([quot, jnp.zeros((128 - TOK, 128), F32)], axis=0).T[0:TOP, :]

    def gather_home(s, chained=False):
        bulk(pr_r.at[s])
        mx, tg = sums_of(s)
        if chained:
            leave(s - 1).wait_recv()
            mx += zx[s - 1, 0:TOK, :].astype(F32)
            tg += zx[s - 1, TOK : 2 * TOK, :].astype(F32)
        zs[s, 0:TOK, :] = mx.astype(BF)
        zs[s, TOK : 2 * TOK, :] = tg.astype(BF)
        leave(s).start()
        zq[s] = inner_of(s)
        leave_inner(s).start()

    bulk(pd_r.at[turn(0)])
    exchange(turn(0)).start()

    @pl.loop(0, NZ)
    def _(i):
        @pl.when(i < NZ - 1)
        def _():
            bulk(pd_r.at[turn(i + 1)])
            exchange(turn(i + 1)).start()

        exchange(turn(i)).wait()
        expert_step(i)

        @pl.when(i > 0)
        def _():
            go_home(i - 1)

        @pl.when((i > 2) * (i < NZ - 1))
        def _():
            gather_home(turn(i - 3))

    go_home(NZ - 1)

    def weights(i):
        f = pl.ds(pl.multiple_of(i * 256, 256), 256)
        g = dot(recv[:, 0:half, f].reshape(NZ * half, 256), dgu[...], 0, 0)
        gwg[f, :] = g[:, 0:HID].astype(BF)
        gwu[f, :] = g[:, HID : 2 * HID].astype(BF)
        gwd[:, f] = dot(hid[...], recv[:, half:ROWS, f].reshape(NZ * half, 256), 0, 0).astype(BF)

    pl.loop(0, 3)(weights)
    gather_home(5, chained=True)
    pl.loop(3, 6)(weights)
    gather_home(6, chained=True)
    pl.loop(6, D // 256)(weights)
    stores = [
        pltpu.make_async_copy(src, dst.at[0], o_sem.at[i])
        for i, (src, dst) in enumerate(((gwg, gwg_o), (gwu, gwu_o), (gwd, gwd_o)))
    ]
    for c in stores:
        c.start()
    gather_home(7, chained=True)

    quot = jnp.zeros((TOP, 128), F32)
    for s in range(1, NZ):
        leave_inner(s).wait_recv()
        quot += zqx[s]
    total = jnp.zeros((2 * TOK, HALF), F32)
    for s in (1, 2, 3):
        leave(s).wait_recv()
        total += zx[s].astype(F32)
    bulk(pr_r.at[0])
    mx, tg = sums_of(0)
    leave(NZ - 1).wait_recv()
    total += zx[NZ - 1].astype(F32)
    fin[0:TOK, :] = (total[0:TOK] + mx).astype(BF)
    fin[TOK : 2 * TOK, :] = (total[TOK : 2 * TOK] + tg).astype(BF)
    last = [
        remote(src, dst, f_s.at[i], f_r.at[i], partner)
        for i, (src, dst) in enumerate(((fin, finr), (finq, finqr)))
    ]
    last[0].start()
    quot += inner_of(0)
    finq[...] = quot
    last[1].start()
    mixed_o[:, mine] = fin[0:TOK, :]
    tgrad_o[:, mine] = fin[TOK : 2 * TOK, :]
    for c in last:
        c.wait()
    mixed_o[:, other] = finr[0:TOK, :]
    tgrad_o[:, other] = finr[TOK : 2 * TOK, :]
    gg_o[...] = (quot + finqr[...])[:, 0:TOK]

    for c in hops:
        c.wait_send()
    for s in range(NZ):
        bulk(pd_s.at[s])
        bulk(pr_s.at[s])
        if s:
            leave(s).wait_send()
            leave_inner(s).wait_send()
    for c in stores:
        c.wait()


def place(*refs):
    src, dst, sem = refs[0:6], refs[6:12], refs[12]
    copies = []
    for i in range(6):
        copies.append(pltpu.make_async_copy(src[i], dst[i], sem.at[i]))
        copies[-1].start()
    for c in copies:
        c.wait()


def body(tokens, routes, gates, cotangent, w_gate, w_up, w_down):
    vm = pl.BlockSpec(memory_space=pltpu.VMEM)
    hbm = pl.BlockSpec(memory_space=pl.ANY)
    dma = pltpu.SemaphoreType.DMA
    shapes = (
        jax.ShapeDtypeStruct((TOK, D), BF),
        jax.ShapeDtypeStruct((TOK, D), BF),
        jax.ShapeDtypeStruct((TOP, TOK), F32),
        jax.ShapeDtypeStruct((1, D, HID), BF),
        jax.ShapeDtypeStruct((1, D, HID), BF),
        jax.ShapeDtypeStruct((1, HID, D), BF),
    )
    outs = pl.pallas_call(
        kernel,
        out_shape=shapes,
        in_specs=[pl.BlockSpec(memory_space=pltpu.HBM)] * 7,
        out_specs=(vm, vm, vm, hbm, hbm, hbm),
        scratch_shapes=[
            pltpu.VMEM((TOP, TOK), jnp.int32),
            pltpu.VMEM((TOP, TOK), F32),
            pltpu.VMEM((NZ, 2 * TOK, HALF), BF),
            pltpu.VMEM((NZ, TOK, 128), F32),
            pltpu.VMEM((NZ, 4 * TOK, ROWS), BF),
            pltpu.VMEM((NZ, ROWS, HALF), BF),
            pltpu.VMEM((NZ, ROWS, D), BF),
            pltpu.VMEM((D, HID), BF),
            pltpu.VMEM((D, HID), BF),
            pltpu.VMEM((HID, D), BF),
            pltpu.VMEM((2, ROWS, HALF), F32),
            pltpu.VMEM((2, ROWS, HALF), BF),
            pltpu.VMEM((4, ROWS, HALF), BF),
            pltpu.VMEM((NZ, ROWS, HALF), BF),
            pltpu.VMEM((NZ, ROWS, HALF), BF),
            pltpu.VMEM((NZ, 2 * TOK, HALF), BF),
            pltpu.VMEM((NZ, TOP, 128), F32),
            pltpu.VMEM((NZ, 2 * TOK, HALF), BF),
            pltpu.VMEM((NZ, TOP, 128), F32),
            pltpu.VMEM((2 * TOK, HALF), BF),
            pltpu.VMEM((2 * TOK, HALF), BF),
            pltpu.VMEM((TOP, 128), F32),
            pltpu.VMEM((TOP, 128), F32),
            pltpu.VMEM((NZ * ROWS // 2, HID), BF),
            pltpu.VMEM((NZ * ROWS // 2, 2 * HID), BF),
            pltpu.VMEM((D, HID), BF),
            pltpu.VMEM((D, HID), BF),
            pltpu.VMEM((HID, D), BF),
            dma((4,)),
            dma((3,)),
            dma((3, 2, 4)),
            dma((3, 2, 4)),
        ]
        + [dma((NZ,))] * 12
        + [dma((2,)), dma((2,)), dma((3,))],
        compiler_params=pltpu.CompilerParams(
            collective_id=0, has_side_effects=True, vmem_limit_bytes=48 << 20
        ),
        name="moe",
    )(*[pltpu.with_memory_space_constraint(a, pltpu.HBM) for a in (tokens, cotangent, routes.T, gates.T, w_gate, w_up, w_down)])
    outs = pl.pallas_call(
        place,
        out_shape=shapes,
        in_specs=[vm] * 6,
        out_specs=[hbm] * 6,
        scratch_shapes=[dma((6,))],
        compiler_params=pltpu.CompilerParams(vmem_limit_bytes=8 << 20),
        name="place",
    )(*[pltpu.with_memory_space_constraint(o, pltpu.VMEM) for o in outs])
    return (outs[0], outs[1], outs[2].T) + tuple(outs[3:])


def solution(mesh):
    placed = (
        P("expert", None),
        P("expert", None),
        P("expert", None),
        P("expert", None),
        P("expert", None, "half"),
        P("expert", None, "half"),
        P("expert", "half", None),
    )
    return jax.shard_map(
        body,
        mesh=mesh,
        in_specs=placed,
        out_specs=(
            P("expert", None),
            P("expert", None),
            P("expert", None),
            P("expert", None, "half"),
            P("expert", None, "half"),
            P("expert", "half", None),
        ),
        check_vma=False,
    )
```

```python
import jax
import jax.numpy as jnp
from jax import lax
from jax.experimental import pallas as pl
from jax.experimental.pallas import tpu as pltpu
from jax.sharding import PartitionSpec as P

MESH = pl.DeviceIdType.MESH
NX, NZ, NY = 4, 8, 4
PLANE = NX * NY
TOK = 64
D = 2048
HALF = D // 2
HID = 384
TOP = 8
CAP = 8
ROWS = PLANE * 2 * CAP
ORDER = (3, 4, 5, 2, 6, 1, 7, 0)
FAR_FIRST = (10, 6, 9, 11, 14, 5, 7, 13, 15, 2, 8, 1, 4, 3, 12)
BF = jnp.bfloat16
F32 = jnp.float32


def dot(a, b, ca, cb):
    return lax.dot_general(a, b, (((ca,), (cb,)), ((), ())), preferred_element_type=F32)


def kernel(
    tok, cot, routes, gates, wg_h, wu_h, wd_h,
    mixed_o, tgrad_o, gg_o, gwg_o, gwu_o, gwd_o,
    routes_v, gates_v, gath, meta, mats, sel, recv, wg, wu, wd, own, psend, precv, ret, rret,
    acc, zs, zq, zx, zqx, fin, finr, finq, finqr, hid, dgu, gwg, gwu, gwd,
    i_sem, w_sem, zt_s, zt_r, pd_s, pd_r, cx_s, cx_r, px_s, px_r, pr_s, pr_r,
    zr_s, zr_r, zq_s, zq_r, f_s, f_r, o_sem,
):
    e = lax.axis_index("expert")
    h = lax.axis_index("half")
    x, z, y = e // (NZ * NY), (e // NY) % NZ, e % NY
    me = x * NY + y
    mine = pl.ds(pl.multiple_of(h * HALF, HALF), HALF)
    other = pl.ds(pl.multiple_of((1 - h) * HALF, HALF), HALF)

    def at_z(dz):
        return ((x * NZ + (z + dz) % NZ) * NY + y, h)

    def in_plane(r):
        xx = (x + r // NY) % NX
        yy = (y + r % NY) % NY
        return ((xx * NZ + z) * NY + yy, h), xx * NY + yy

    partner = (e, 1 - h)

    def remote(src, dst, ss, rs, dev):
        return pltpu.make_async_remote_copy(
            src_ref=src, dst_ref=dst, send_sem=ss, recv_sem=rs, device_id=dev, device_id_type=MESH
        )

    firsts = [
        pltpu.make_async_copy(tok.at[:, mine], gath.at[z, pl.ds(0, TOK)], i_sem.at[0]),
        pltpu.make_async_copy(cot.at[:, mine], gath.at[z, pl.ds(TOK, TOK)], i_sem.at[1]),
        pltpu.make_async_copy(routes, routes_v, i_sem.at[2]),
        pltpu.make_async_copy(gates, gates_v, i_sem.at[3]),
    ]
    for c in firsts:
        c.start()
    loads = [
        pltpu.make_async_copy(src.at[0], dst, w_sem.at[i])
        for i, (src, dst) in enumerate(((wg_h, wg), (wu_h, wu), (wd_h, wd)))
    ]
    for c in loads:
        c.start()

    barrier = pltpu.get_barrier_semaphore()
    for r in range(1, PLANE):
        pl.semaphore_signal(barrier, inc=1, device_id=in_plane(r)[0], device_id_type=MESH)
    for r in range(1, NZ):
        pl.semaphore_signal(barrier, inc=1, device_id=at_z(r), device_id_type=MESH)
    pl.semaphore_signal(barrier, inc=1, device_id=partner, device_id_type=MESH)

    for c in firsts:
        c.wait()
    flat = jnp.concatenate([routes_v[...].astype(F32), gates_v[...]], axis=0)
    flat = jnp.concatenate([flat, jnp.zeros((112, TOK), F32)], axis=0)
    meta[z] = flat.T

    lane = lax.broadcasted_iota(jnp.int32, (TOK, ROWS), 1)
    expert = lane // (2 * CAP)
    ids = ((expert // NY * NZ + z) * NY + expert % NY).astype(F32)
    slot = (lane % CAP).astype(F32)
    kind = ((lane // CAP) % 2).astype(F32)

    def select(s):
        zz = (z + s) % NZ
        info = meta[zz]
        named = jnp.zeros((TOK, ROWS), F32)
        weight = jnp.zeros((TOK, ROWS), F32)
        for k in range(TOP):
            hit = info[:, k : k + 1] == ids
            named = jnp.where(hit, 1.0, named)
            weight = jnp.where(hit, info[:, TOP + k : TOP + k + 1], weight)
        r0 = lax.broadcasted_iota(jnp.int32, (TOK, TOK), 0)
        r1 = lax.broadcasted_iota(jnp.int32, (TOK, TOK), 1)
        before = jnp.where(r1 < r0, 1.0, 0.0).astype(BF)
        placed = dot(before, named.astype(BF), 1, 0)
        one = jnp.where(placed == slot, named, 0.0)
        out_one = one * kind
        weight = out_one * weight
        high = weight.astype(BF)
        low = (weight - high.astype(F32)).astype(BF)
        mats[s, 0:TOK, :] = (one - out_one).astype(BF)
        mats[s, TOK : 2 * TOK, :] = high
        mats[s, 2 * TOK : 3 * TOK, :] = low
        mats[s, 3 * TOK : 4 * TOK, :] = out_one.astype(BF)
        source = jnp.concatenate([gath[zz], gath[zz, TOK : 2 * TOK, :]], axis=0)
        sel[s] = dot(mats[s, 0 : 3 * TOK, :], source, 0, 0).astype(BF)

    select(0)
    pl.semaphore_wait(barrier, PLANE - 1 + NZ - 1 + 1)

    def hop(stream, way, d, src_z):
        ref = meta.at[src_z] if stream == 2 else gath.at[src_z, pl.ds(stream * TOK, TOK)]
        return remote(
            ref, ref, zt_s.at[stream, way, d - 1], zt_r.at[stream, way, d - 1],
            at_z(1 if way == 0 else NZ - 1),
        )

    reach = ((4, 3), (3, 4), (4, 3))
    hops = []
    for stream in (2, 0, 1):
        for way in (1, 0):
            c = hop(stream, way, 1, z)
            c.start()
            hops.append(c)

    def arrive(d):
        for stream in (2, 0, 1):
            for way in (1, 0):
                if d <= reach[stream][way]:
                    src = (z + NZ - d) % NZ if way == 0 else (z + d) % NZ
                    hop(stream, way, d, src).wait_recv()
                    if d + 1 <= reach[stream][way]:
                        c = hop(stream, way, d + 1, src)
                        c.start()
                        hops.append(c)

    def block(p):
        return pl.ds(pl.multiple_of(p * 2 * CAP, 2 * CAP), 2 * CAP)

    def dispatch(s):
        for r in FAR_FIRST:
            dev, p = in_plane(r)
            remote(
                sel.at[s, block(p)], recv.at[s, block(me), mine], pd_s.at[s], pd_r.at[s], dev
            ).start()
        recv[s, block(me), mine] = sel[s, block(me), :]

    def bulk(sem):
        blocks = sel.at[0, pl.ds(0, ROWS - 2 * CAP)]
        pltpu.make_async_copy(blocks, blocks, sem).wait()

    dispatch(0)
    for s in range(1, NZ):
        if s <= 4:
            arrive(s)
        select(s)
        dispatch(s)

    for c in loads:
        c.wait()

    def exchange(s):
        return remote(
            recv.at[s, :, mine], recv.at[s, :, mine], cx_s.at[s], cx_r.at[s], partner
        )

    def turn(i):
        bits = (i % 2, (i // 2) % 2, i // 4)
        total = 0
        for m in range(NZ):
            part = sum(
                (-1) ** bin(m ^ k).count("1") * ORDER[k] for k in range(NZ) if k & m == k
            )
            if part:
                for b in range(3):
                    if m >> b & 1:
                        part = part * bits[b]
                total = total + part
        return total

    def partial(i):
        return remote(psend.at[i % 2], precv.at[i % 4], px_s.at[i], px_r.at[i], partner)

    half = ROWS // 2

    def expert_step(i):
        s = turn(i)
        at = pl.ds(pl.multiple_of(s * half, half), half)
        for q in range(4):
            f = slice(q * 512, (q + 1) * 512)
            v = recv[s, :, f].astype(F32).reshape(PLANE, 2, CAP, 512)
            recv[s, 0:half, f] = v[:, 0].reshape(half, 512).astype(BF)
            recv[s, half:ROWS, f] = v[:, 1].reshape(half, 512).astype(BF)
        r = recv[s, 0:half, :]
        pre_gate = dot(r, wg[...], 1, 0)
        pre_up = dot(r, wu[...], 1, 0)
        back = dot(recv[s, half:ROWS, :], wd[...], 1, 1)
        sigma = jax.nn.sigmoid(pre_gate)
        hidden = (pre_gate * sigma * pre_up).astype(BF)
        d_up = (back * pre_gate * sigma).astype(BF)
        d_gate = (back * pre_up * sigma * (1.0 + pre_gate * (1.0 - sigma))).astype(BF)
        hid[at, :] = hidden
        dgu[at, 0:HID] = d_gate
        dgu[at, HID : 2 * HID] = d_up
        p = i % 2
        psend[p, 0:half, :] = (dot(d_gate, wg[other, :], 1, 1) + dot(d_up, wu[other, :], 1, 1)).astype(BF)
        psend[p, half:ROWS, :] = dot(hidden, wd[:, other], 1, 0).astype(BF)
        partial(i).start()
        own[p, 0:half, :] = dot(d_gate, wg[mine, :], 1, 1) + dot(d_up, wu[mine, :], 1, 1)
        own[p, half:ROWS, :] = dot(hidden, wd[:, mine], 1, 0)

    def go_home(i):
        s = turn(i)
        partial(i).wait()
        v = own[i % 2] + precv[i % 4].astype(F32)
        v = jnp.concatenate(
            [v[0:half].reshape(PLANE, 1, CAP, HALF), v[half:ROWS].reshape(PLANE, 1, CAP, HALF)], axis=1
        )
        ret[s] = v.reshape(ROWS, HALF).astype(BF)
        for k in FAR_FIRST:
            dev, p = in_plane(k)
            remote(ret.at[s, block(p)], rret.at[s, block(me)], pr_s.at[s], pr_r.at[s], dev).start()
        rret[s, block(me), :] = ret[s, block(me), :]

    lane128 = lax.broadcasted_iota(jnp.int32, (TOK, 128), 1)

    def leave(s):
        dz = s + (s // 4) * (NZ - 1 - s)
        return remote(zs.at[s], zx.at[s], zr_s.at[s], zr_r.at[s], at_z(dz))

    def leave_inner(s):
        return remote(zq.at[s], zqx.at[s], zq_s.at[s], zq_r.at[s], at_z(s))

    def sums_of(s):
        sums = dot(mats[s, 0 : 3 * TOK, :], rret[s], 1, 0)
        return sums[TOK : 2 * TOK] + sums[2 * TOK : 3 * TOK], sums[0:TOK]

    def inner_of(s):
        zz = (z + s) % NZ
        inner = dot(gath[zz, TOK : 2 * TOK, :], rret[s], 1, 1)
        inner = inner * mats[s, 3 * TOK : 4 * TOK, :].astype(F32)
        info = meta[zz]
        quot = jnp.zeros((TOK, 128), F32)
        for k in range(TOP):
            hit = info[:, k : k + 1] == ids
            v = jnp.sum(jnp.where(hit, inner, 0.0), axis=1, keepdims=True)
            quot = jnp.where(lane128 == k, v, quot)
        return jnp.concatenate([quot, jnp.zeros((128 - TOK, 128), F32)], axis=0).T[0:TOP, :]

    def gather_home(i, chained):
        s = turn(i)
        bulk(pr_r.at[s])
        mx, tg = sums_of(s)
        acc[0:TOK, :] = mx
        acc[TOK : 2 * TOK, :] = tg

        @pl.when(chained)
        def _():
            leave(s - 1).wait_recv()
            acc[...] += zx[s - 1].astype(F32)

        zs[s] = acc[...].astype(BF)
        leave(s).start()
        zq[s] = inner_of(s)
        leave_inner(s).start()

    bulk(pd_r.at[turn(0)])
    exchange(turn(0)).start()

    @pl.loop(0, NZ)
    def _(i):
        exchange(turn(i)).wait()
        expert_step(i)

        @pl.when(i > 0)
        def _():
            go_home(i - 1)

        @pl.when(i < NZ - 1)
        def _():
            bulk(pd_r.at[turn(i + 1)])
            exchange(turn(i + 1)).start()

        @pl.when(i > 2)
        def _():
            gather_home(i - 3, (i == 5) | (i == 7))

    go_home(NZ - 1)

    def weights(i):
        f = pl.ds(pl.multiple_of(i * 256, 256), 256)
        g = dot(recv[:, 0:half, f].reshape(NZ * half, 256), dgu[...], 0, 0)
        gwg[f, :] = g[:, 0:HID].astype(BF)
        gwu[f, :] = g[:, HID : 2 * HID].astype(BF)
        gwd[:, f] = dot(hid[...], recv[:, half:ROWS, f].reshape(NZ * half, 256), 0, 0).astype(BF)

    gather_home(5, False)
    pl.loop(0, 4)(weights)
    gather_home(6, True)
    pl.loop(4, D // 256)(weights)
    stores = [
        pltpu.make_async_copy(src, dst.at[0], o_sem.at[i])
        for i, (src, dst) in enumerate(((gwg, gwg_o), (gwu, gwu_o), (gwd, gwd_o)))
    ]
    for c in stores:
        c.start()
    quot = jnp.zeros((TOP, 128), F32)
    for s in range(1, NZ):
        leave_inner(s).wait_recv()
        quot += zqx[s]
    total = jnp.zeros((2 * TOK, HALF), F32)
    for s in (1, 2, 3):
        leave(s).wait_recv()
        total += zx[s].astype(F32)
    bulk(pr_r.at[0])
    mx, tg = sums_of(0)
    leave(NZ - 1).wait_recv()
    total += zx[NZ - 1].astype(F32)
    fin[0:TOK, :] = (total[0:TOK] + mx).astype(BF)
    fin[TOK : 2 * TOK, :] = (total[TOK : 2 * TOK] + tg).astype(BF)
    last = [
        remote(src, dst, f_s.at[i], f_r.at[i], partner)
        for i, (src, dst) in enumerate(((fin, finr), (finq, finqr)))
    ]
    last[0].start()
    quot += inner_of(0)
    finq[...] = quot
    last[1].start()
    mixed_o[:, mine] = fin[0:TOK, :]
    tgrad_o[:, mine] = fin[TOK : 2 * TOK, :]
    for c in last:
        c.wait()
    mixed_o[:, other] = finr[0:TOK, :]
    tgrad_o[:, other] = finr[TOK : 2 * TOK, :]
    gg_o[...] = (quot + finqr[...])[:, 0:TOK]

    for c in hops:
        c.wait_send()
    for s in range(NZ):
        bulk(pd_s.at[s])
        bulk(pr_s.at[s])
        if s:
            leave(s).wait_send()
            leave_inner(s).wait_send()
    for c in stores:
        c.wait()


def place(*refs):
    src, dst, sem = refs[0:6], refs[6:12], refs[12]
    copies = []
    for i in range(6):
        copies.append(pltpu.make_async_copy(src[i], dst[i], sem.at[i]))
        copies[-1].start()
    for c in copies:
        c.wait()


def body(tokens, routes, gates, cotangent, w_gate, w_up, w_down):
    vm = pl.BlockSpec(memory_space=pltpu.VMEM)
    hbm = pl.BlockSpec(memory_space=pl.ANY)
    dma = pltpu.SemaphoreType.DMA
    shapes = (
        jax.ShapeDtypeStruct((TOK, D), BF),
        jax.ShapeDtypeStruct((TOK, D), BF),
        jax.ShapeDtypeStruct((TOP, TOK), F32),
        jax.ShapeDtypeStruct((1, D, HID), BF),
        jax.ShapeDtypeStruct((1, D, HID), BF),
        jax.ShapeDtypeStruct((1, HID, D), BF),
    )
    outs = pl.pallas_call(
        kernel,
        out_shape=shapes,
        in_specs=[pl.BlockSpec(memory_space=pltpu.HBM)] * 7,
        out_specs=(vm, vm, vm, hbm, hbm, hbm),
        scratch_shapes=[
            pltpu.VMEM((TOP, TOK), jnp.int32),
            pltpu.VMEM((TOP, TOK), F32),
            pltpu.VMEM((NZ, 2 * TOK, HALF), BF),
            pltpu.VMEM((NZ, TOK, 128), F32),
            pltpu.VMEM((NZ, 4 * TOK, ROWS), BF),
            pltpu.VMEM((NZ, ROWS, HALF), BF),
            pltpu.VMEM((NZ, ROWS, D), BF),
            pltpu.VMEM((D, HID), BF),
            pltpu.VMEM((D, HID), BF),
            pltpu.VMEM((HID, D), BF),
            pltpu.VMEM((2, ROWS, HALF), F32),
            pltpu.VMEM((2, ROWS, HALF), BF),
            pltpu.VMEM((4, ROWS, HALF), BF),
            pltpu.VMEM((NZ, ROWS, HALF), BF),
            pltpu.VMEM((NZ, ROWS, HALF), BF),
            pltpu.VMEM((2 * TOK, HALF), F32),
            pltpu.VMEM((NZ, 2 * TOK, HALF), BF),
            pltpu.VMEM((NZ, TOP, 128), F32),
            pltpu.VMEM((NZ, 2 * TOK, HALF), BF),
            pltpu.VMEM((NZ, TOP, 128), F32),
            pltpu.VMEM((2 * TOK, HALF), BF),
            pltpu.VMEM((2 * TOK, HALF), BF),
            pltpu.VMEM((TOP, 128), F32),
            pltpu.VMEM((TOP, 128), F32),
            pltpu.VMEM((NZ * ROWS // 2, HID), BF),
            pltpu.VMEM((NZ * ROWS // 2, 2 * HID), BF),
            pltpu.VMEM((D, HID), BF),
            pltpu.VMEM((D, HID), BF),
            pltpu.VMEM((HID, D), BF),
            dma((4,)),
            dma((3,)),
            dma((3, 2, 4)),
            dma((3, 2, 4)),
        ]
        + [dma((NZ,))] * 12
        + [dma((2,)), dma((2,)), dma((3,))],
        compiler_params=pltpu.CompilerParams(
            collective_id=0, has_side_effects=True, vmem_limit_bytes=48 << 20
        ),
        name="moe",
    )(*[pltpu.with_memory_space_constraint(a, pltpu.HBM) for a in (tokens, cotangent, routes.T, gates.T, w_gate, w_up, w_down)])
    outs = pl.pallas_call(
        place,
        out_shape=shapes,
        in_specs=[vm] * 6,
        out_specs=[hbm] * 6,
        scratch_shapes=[dma((6,))],
        compiler_params=pltpu.CompilerParams(vmem_limit_bytes=8 << 20),
        name="place",
    )(*[pltpu.with_memory_space_constraint(o, pltpu.VMEM) for o in outs])
    return (outs[0], outs[1], outs[2].T) + tuple(outs[3:])


def solution(mesh):
    placed = (
        P("expert", None),
        P("expert", None),
        P("expert", None),
        P("expert", None),
        P("expert", None, "half"),
        P("expert", None, "half"),
        P("expert", "half", None),
    )
    return jax.shard_map(
        body,
        mesh=mesh,
        in_specs=placed,
        out_specs=(
            P("expert", None),
            P("expert", None),
            P("expert", None),
            P("expert", None, "half"),
            P("expert", None, "half"),
            P("expert", "half", None),
        ),
        check_vma=False,
    )
```

```python
import jax
import jax.numpy as jnp
from jax import lax
from jax.experimental import pallas as pl
from jax.experimental.pallas import tpu as pltpu
from jax.sharding import PartitionSpec as P

MESH = pl.DeviceIdType.MESH
NX, NZ, NY = 4, 8, 4
PLANE = NX * NY
TOK = 64
D = 2048
HALF = D // 2
HID = 384
TOP = 8
CAP = 8
ROWS = PLANE * 2 * CAP
OUTWARD = (0, 1, 7, 2, 3, 4, 5, 6)
ORDER = (2, 3, 4, 5, 6, 1, 7, 0)
FAR_FIRST = (10, 6, 9, 11, 14, 5, 7, 13, 15, 2, 8, 1, 4, 3, 12)
BF = jnp.bfloat16
F32 = jnp.float32


def dot(a, b, ca, cb):
    return lax.dot_general(a, b, (((ca,), (cb,)), ((), ())), preferred_element_type=F32)


def kernel(
    tok, cot, routes, gates, wg_h, wu_h, wd_h,
    mixed_o, tgrad_o, gg_o, gwg_o, gwu_o, gwd_o,
    routes_v, gates_v, gath, meta, mats, sel, recv, wg, wu, wd, own, psend, precv, ret, rret,
    acc, zs, zq, zx, zqx, fin, finr, finq, finqr, hid, dgu, gwg, gwu, gwd,
    i_sem, w_sem, zt_s, zt_r, pd_s, pd_r, cx_s, cx_r, px_s, px_r, pr_s, pr_r,
    zr_s, zr_r, zq_s, zq_r, f_s, f_r, o_sem,
):
    e = lax.axis_index("expert")
    h = lax.axis_index("half")
    x, z, y = e // (NZ * NY), (e // NY) % NZ, e % NY
    me = x * NY + y
    mine = pl.ds(pl.multiple_of(h * HALF, HALF), HALF)
    other = pl.ds(pl.multiple_of((1 - h) * HALF, HALF), HALF)

    def at_z(dz):
        return ((x * NZ + (z + dz) % NZ) * NY + y, h)

    def in_plane(r):
        xx = (x + r // NY) % NX
        yy = (y + r % NY) % NY
        return ((xx * NZ + z) * NY + yy, h), xx * NY + yy

    partner = (e, 1 - h)

    def remote(src, dst, ss, rs, dev):
        return pltpu.make_async_remote_copy(
            src_ref=src, dst_ref=dst, send_sem=ss, recv_sem=rs, device_id=dev, device_id_type=MESH
        )

    firsts = [
        pltpu.make_async_copy(tok.at[:, mine], gath.at[z, pl.ds(0, TOK)], i_sem.at[0]),
        pltpu.make_async_copy(cot.at[:, mine], gath.at[z, pl.ds(TOK, TOK)], i_sem.at[1]),
        pltpu.make_async_copy(routes, routes_v, i_sem.at[2]),
        pltpu.make_async_copy(gates, gates_v, i_sem.at[3]),
    ]
    for c in firsts:
        c.start()
    loads = [
        pltpu.make_async_copy(src.at[0], dst, w_sem.at[i])
        for i, (src, dst) in enumerate(((wg_h, wg), (wu_h, wu), (wd_h, wd)))
    ]
    for c in loads:
        c.start()

    barrier = pltpu.get_barrier_semaphore()
    for r in range(1, PLANE):
        pl.semaphore_signal(barrier, inc=1, device_id=in_plane(r)[0], device_id_type=MESH)
    for r in range(1, NZ):
        pl.semaphore_signal(barrier, inc=1, device_id=at_z(r), device_id_type=MESH)
    pl.semaphore_signal(barrier, inc=1, device_id=partner, device_id_type=MESH)

    for c in firsts:
        c.wait()
    flat = jnp.concatenate([routes_v[...].astype(F32), gates_v[...]], axis=0)
    meta[z] = jnp.concatenate([flat, jnp.zeros((2 * TOP, 128 - TOK), F32)], axis=1)

    lane = lax.broadcasted_iota(jnp.int32, (TOK, ROWS), 1)
    expert = lane // (2 * CAP)
    ids = ((expert // NY * NZ + z) * NY + expert % NY).astype(F32)
    slot = (lane % CAP).astype(F32)
    kind = ((lane // CAP) % 2).astype(F32)

    def select(s):
        zz = (z + s) % NZ
        info = meta[zz].T[0:TOK]
        named = jnp.zeros((TOK, ROWS), F32)
        weight = jnp.zeros((TOK, ROWS), F32)
        for k in range(TOP):
            hit = info[:, k : k + 1] == ids
            named = jnp.where(hit, 1.0, named)
            weight = jnp.where(hit, info[:, TOP + k : TOP + k + 1], weight)
        r0 = lax.broadcasted_iota(jnp.int32, (TOK, TOK), 0)
        r1 = lax.broadcasted_iota(jnp.int32, (TOK, TOK), 1)
        before = jnp.where(r1 < r0, 1.0, 0.0).astype(BF)
        placed = dot(before, named.astype(BF), 1, 0)
        one = jnp.where(placed == slot, named, 0.0)
        out_one = one * kind
        weight = out_one * weight
        high = weight.astype(BF)
        low = (weight - high.astype(F32)).astype(BF)
        mats[s, 0:TOK, :] = (one - out_one).astype(BF)
        mats[s, TOK : 2 * TOK, :] = high
        mats[s, 2 * TOK : 3 * TOK, :] = low
        mats[s, 3 * TOK : 4 * TOK, :] = out_one.astype(BF)
        source = jnp.concatenate([gath[zz], gath[zz, TOK : 2 * TOK, :]], axis=0)
        sel[s] = dot(mats[s, 0 : 3 * TOK, :], source, 0, 0).astype(BF)

    pl.semaphore_wait(barrier, PLANE - 1 + NZ - 1 + 1)

    def hop(stream, way, d, src_z):
        ref = meta.at[src_z] if stream == 2 else gath.at[src_z, pl.ds(stream * TOK, TOK)]
        return remote(
            ref, ref, zt_s.at[stream, way, d - 1], zt_r.at[stream, way, d - 1],
            at_z(1 if way == 0 else NZ - 1),
        )

    reach = ((4, 3), (3, 4), (4, 3))
    hops = []
    for stream in (2, 0, 1):
        for way in (1, 0):
            c = hop(stream, way, 1, z)
            c.start()
            hops.append(c)

    def arrive(d):
        for stream in (2, 0, 1):
            for way in (1, 0):
                if d <= reach[stream][way]:
                    src = (z + NZ - d) % NZ if way == 0 else (z + d) % NZ
                    hop(stream, way, d, src).wait_recv()
                    if d + 1 <= reach[stream][way]:
                        c = hop(stream, way, d + 1, src)
                        c.start()
                        hops.append(c)

    def block(p):
        return pl.ds(pl.multiple_of(p * 2 * CAP, 2 * CAP), 2 * CAP)

    def dispatch(s):
        for r in FAR_FIRST:
            dev, p = in_plane(r)
            remote(
                sel.at[s, block(p)], recv.at[s, block(me), mine], pd_s.at[s], pd_r.at[s], dev
            ).start()
        recv[s, block(me), mine] = sel[s, block(me), :]

    def bulk(sem):
        blocks = sel.at[0, pl.ds(0, ROWS - 2 * CAP)]
        pltpu.make_async_copy(blocks, blocks, sem).wait()

    for s in OUTWARD:
        if 1 <= s <= 4:
            arrive(s)
        select(s)
        dispatch(s)

    for c in loads:
        c.wait()

    def exchange(s):
        return remote(
            recv.at[s, :, mine], recv.at[s, :, mine], cx_s.at[s], cx_r.at[s], partner
        )

    def turn(i):
        bits = (i % 2, (i // 2) % 2, i // 4)
        total = 0
        for m in range(NZ):
            part = sum(
                (-1) ** bin(m ^ k).count("1") * ORDER[k] for k in range(NZ) if k & m == k
            )
            if part:
                for b in range(3):
                    if m >> b & 1:
                        part = part * bits[b]
                total = total + part
        return total

    def partial(i):
        return remote(psend.at[i % 2], precv.at[i % 4], px_s.at[i], px_r.at[i], partner)

    half = ROWS // 2

    def expert_step(i):
        s = turn(i)
        at = pl.ds(pl.multiple_of(s * half, half), half)
        for q in range(4):
            f = slice(q * 512, (q + 1) * 512)
            v = recv[s, :, f].astype(F32).reshape(PLANE, 2, CAP, 512)
            recv[s, 0:half, f] = v[:, 0].reshape(half, 512).astype(BF)
            recv[s, half:ROWS, f] = v[:, 1].reshape(half, 512).astype(BF)
        r = recv[s, 0:half, :]
        pre_gate = dot(r, wg[...], 1, 0)
        pre_up = dot(r, wu[...], 1, 0)
        back = dot(recv[s, half:ROWS, :], wd[...], 1, 1)
        sigma = jax.nn.sigmoid(pre_gate)
        hidden = (pre_gate * sigma * pre_up).astype(BF)
        d_up = (back * pre_gate * sigma).astype(BF)
        d_gate = (back * pre_up * sigma * (1.0 + pre_gate * (1.0 - sigma))).astype(BF)
        hid[at, :] = hidden
        dgu[at, 0:HID] = d_gate
        dgu[at, HID : 2 * HID] = d_up
        p = i % 2
        psend[p, 0:half, :] = (dot(d_gate, wg[other, :], 1, 1) + dot(d_up, wu[other, :], 1, 1)).astype(BF)
        psend[p, half:ROWS, :] = dot(hidden, wd[:, other], 1, 0).astype(BF)
        partial(i).start()
        own[p, 0:half, :] = dot(d_gate, wg[mine, :], 1, 1) + dot(d_up, wu[mine, :], 1, 1)
        own[p, half:ROWS, :] = dot(hidden, wd[:, mine], 1, 0)

    def go_home(i):
        s = turn(i)
        partial(i).wait()
        v = own[i % 2] + precv[i % 4].astype(F32)
        v = jnp.concatenate(
            [v[0:half].reshape(PLANE, 1, CAP, HALF), v[half:ROWS].reshape(PLANE, 1, CAP, HALF)], axis=1
        )
        ret[s] = v.reshape(ROWS, HALF).astype(BF)
        for k in FAR_FIRST:
            dev, p = in_plane(k)
            remote(ret.at[s, block(p)], rret.at[s, block(me)], pr_s.at[s], pr_r.at[s], dev).start()
        rret[s, block(me), :] = ret[s, block(me), :]

    lane128 = lax.broadcasted_iota(jnp.int32, (TOK, 128), 1)

    def leave(s):
        dz = s + (s // 4) * (NZ - 1 - s)
        return remote(zs.at[s], zx.at[s], zr_s.at[s], zr_r.at[s], at_z(dz))

    def leave_inner(s):
        return remote(zq.at[s], zqx.at[s], zq_s.at[s], zq_r.at[s], at_z(s))

    def sums_of(s):
        sums = dot(mats[s, 0 : 3 * TOK, :], rret[s], 1, 0)
        return sums[TOK : 2 * TOK] + sums[2 * TOK : 3 * TOK], sums[0:TOK]

    def inner_of(s):
        zz = (z + s) % NZ
        inner = dot(gath[zz, TOK : 2 * TOK, :], rret[s], 1, 1)
        inner = inner * mats[s, 3 * TOK : 4 * TOK, :].astype(F32)
        info = meta[zz].T[0:TOK]
        quot = jnp.zeros((TOK, 128), F32)
        for k in range(TOP):
            hit = info[:, k : k + 1] == ids
            v = jnp.sum(jnp.where(hit, inner, 0.0), axis=1, keepdims=True)
            quot = jnp.where(lane128 == k, v, quot)
        return jnp.concatenate([quot, jnp.zeros((128 - TOK, 128), F32)], axis=0).T[0:TOP, :]

    def gather_home(i, chained):
        s = turn(i)
        bulk(pr_r.at[s])
        mx, tg = sums_of(s)
        acc[0:TOK, :] = mx
        acc[TOK : 2 * TOK, :] = tg

        @pl.when(chained)
        def _():
            leave(s - 1).wait_recv()
            acc[...] += zx[s - 1].astype(F32)

        zs[s] = acc[...].astype(BF)
        leave(s).start()
        zq[s] = inner_of(s)
        leave_inner(s).start()

    bulk(pd_r.at[turn(0)])
    exchange(turn(0)).start()

    @pl.loop(0, NZ)
    def _(i):
        exchange(turn(i)).wait()
        expert_step(i)

        @pl.when(i > 0)
        def _():
            go_home(i - 1)

        @pl.when(i < NZ - 1)
        def _():
            bulk(pd_r.at[turn(i + 1)])
            exchange(turn(i + 1)).start()

        @pl.when(i > 2)
        def _():
            gather_home(i - 3, i > 5)

    go_home(NZ - 1)

    def weights(i):
        f = pl.ds(pl.multiple_of(i * 256, 256), 256)
        g = dot(recv[:, 0:half, f].reshape(NZ * half, 256), dgu[...], 0, 0)
        gwg[f, :] = g[:, 0:HID].astype(BF)
        gwu[f, :] = g[:, HID : 2 * HID].astype(BF)
        gwd[:, f] = dot(hid[...], recv[:, half:ROWS, f].reshape(NZ * half, 256), 0, 0).astype(BF)

    gather_home(5, False)
    pl.loop(0, 4)(weights)
    gather_home(6, True)
    pl.loop(4, D // 256)(weights)
    stores = [
        pltpu.make_async_copy(src, dst.at[0], o_sem.at[i])
        for i, (src, dst) in enumerate(((gwg, gwg_o), (gwu, gwu_o), (gwd, gwd_o)))
    ]
    for c in stores:
        c.start()
    quot = jnp.zeros((TOP, 128), F32)
    for s in range(1, NZ - 1):
        leave_inner(s).wait_recv()
        quot += zqx[s]
    total = jnp.zeros((2 * TOK, HALF), F32)
    for s in (1, 2, 3):
        leave(s).wait_recv()
        total += zx[s].astype(F32)
    for c in hops:
        c.wait_send()
    for s in range(NZ):
        bulk(pd_s.at[s])
    for s in range(1, NZ - 1):
        bulk(pr_s.at[s])
        leave(s).wait_send()
        leave_inner(s).wait_send()
    for c in stores:
        c.wait()
    bulk(pr_r.at[0])
    mx, tg = sums_of(0)
    leave(NZ - 1).wait_recv()
    total += zx[NZ - 1].astype(F32)
    fin[0:TOK, :] = (total[0:TOK] + mx).astype(BF)
    fin[TOK : 2 * TOK, :] = (total[TOK : 2 * TOK] + tg).astype(BF)
    last = [
        remote(src, dst, f_s.at[i], f_r.at[i], partner)
        for i, (src, dst) in enumerate(((fin, finr), (finq, finqr)))
    ]
    last[0].start()
    quot += inner_of(0)
    leave_inner(NZ - 1).wait_recv()
    quot += zqx[NZ - 1]
    finq[...] = quot
    last[1].start()
    mixed_o[:, mine] = fin[0:TOK, :]
    tgrad_o[:, mine] = fin[TOK : 2 * TOK, :]
    for c in last:
        c.wait()
    mixed_o[:, other] = finr[0:TOK, :]
    tgrad_o[:, other] = finr[TOK : 2 * TOK, :]
    gg_o[...] = (quot + finqr[...])[:, 0:TOK]

    bulk(pr_s.at[0])
    bulk(pr_s.at[NZ - 1])
    leave(NZ - 1).wait_send()
    leave_inner(NZ - 1).wait_send()


def place(*refs):
    src, dst, sem = refs[0:6], refs[6:12], refs[12]
    copies = []
    for i in range(6):
        copies.append(pltpu.make_async_copy(src[i], dst[i], sem.at[i]))
        copies[-1].start()
    for c in copies:
        c.wait()


def body(tokens, routes, gates, cotangent, w_gate, w_up, w_down):
    vm = pl.BlockSpec(memory_space=pltpu.VMEM)
    hbm = pl.BlockSpec(memory_space=pl.ANY)
    dma = pltpu.SemaphoreType.DMA
    shapes = (
        jax.ShapeDtypeStruct((TOK, D), BF),
        jax.ShapeDtypeStruct((TOK, D), BF),
        jax.ShapeDtypeStruct((TOP, TOK), F32),
        jax.ShapeDtypeStruct((1, D, HID), BF),
        jax.ShapeDtypeStruct((1, D, HID), BF),
        jax.ShapeDtypeStruct((1, HID, D), BF),
    )
    outs = pl.pallas_call(
        kernel,
        out_shape=shapes,
        in_specs=[pl.BlockSpec(memory_space=pltpu.HBM)] * 7,
        out_specs=(vm, vm, vm, hbm, hbm, hbm),
        scratch_shapes=[
            pltpu.VMEM((TOP, TOK), jnp.int32),
            pltpu.VMEM((TOP, TOK), F32),
            pltpu.VMEM((NZ, 2 * TOK, HALF), BF),
            pltpu.VMEM((NZ, 2 * TOP, 128), F32),
            pltpu.VMEM((NZ, 4 * TOK, ROWS), BF),
            pltpu.VMEM((NZ, ROWS, HALF), BF),
            pltpu.VMEM((NZ, ROWS, D), BF),
            pltpu.VMEM((D, HID), BF),
            pltpu.VMEM((D, HID), BF),
            pltpu.VMEM((HID, D), BF),
            pltpu.VMEM((2, ROWS, HALF), F32),
            pltpu.VMEM((2, ROWS, HALF), BF),
            pltpu.VMEM((4, ROWS, HALF), BF),
            pltpu.VMEM((NZ, ROWS, HALF), BF),
            pltpu.VMEM((NZ, ROWS, HALF), BF),
            pltpu.VMEM((2 * TOK, HALF), F32),
            pltpu.VMEM((NZ, 2 * TOK, HALF), BF),
            pltpu.VMEM((NZ, TOP, 128), F32),
            pltpu.VMEM((NZ, 2 * TOK, HALF), BF),
            pltpu.VMEM((NZ, TOP, 128), F32),
            pltpu.VMEM((2 * TOK, HALF), BF),
            pltpu.VMEM((2 * TOK, HALF), BF),
            pltpu.VMEM((TOP, 128), F32),
            pltpu.VMEM((TOP, 128), F32),
            pltpu.VMEM((NZ * ROWS // 2, HID), BF),
            pltpu.VMEM((NZ * ROWS // 2, 2 * HID), BF),
            pltpu.VMEM((D, HID), BF),
            pltpu.VMEM((D, HID), BF),
            pltpu.VMEM((HID, D), BF),
            dma((4,)),
            dma((3,)),
            dma((3, 2, 4)),
            dma((3, 2, 4)),
        ]
        + [dma((NZ,))] * 12
        + [dma((2,)), dma((2,)), dma((3,))],
        compiler_params=pltpu.CompilerParams(
            collective_id=0, has_side_effects=True, vmem_limit_bytes=48 << 20
        ),
        name="moe",
    )(*[pltpu.with_memory_space_constraint(a, pltpu.HBM) for a in (tokens, cotangent, routes.T, gates.T, w_gate, w_up, w_down)])
    outs = pl.pallas_call(
        place,
        out_shape=shapes,
        in_specs=[vm] * 6,
        out_specs=[hbm] * 6,
        scratch_shapes=[dma((6,))],
        compiler_params=pltpu.CompilerParams(vmem_limit_bytes=8 << 20),
        name="place",
    )(*[pltpu.with_memory_space_constraint(o, pltpu.VMEM) for o in outs])
    return (outs[0], outs[1], outs[2].T) + tuple(outs[3:])


def solution(mesh):
    placed = (
        P("expert", None),
        P("expert", None),
        P("expert", None),
        P("expert", None),
        P("expert", None, "half"),
        P("expert", None, "half"),
        P("expert", "half", None),
    )
    return jax.shard_map(
        body,
        mesh=mesh,
        in_specs=placed,
        out_specs=(
            P("expert", None),
            P("expert", None),
            P("expert", None),
            P("expert", None, "half"),
            P("expert", None, "half"),
            P("expert", "half", None),
        ),
        check_vma=False,
    )
```
